512 devices in a mesh: tile: 128 (over z, y, core), fac: 4 (over x).
Axes of the slice: x: 4, y: 4, z: 16, core: 2. Of those that a mesh axis runs over, the one named last changes fastest.
Arguments:
- panel: float32 [64, 1024, 2048], P('fac', 'tile'), may hold values from -7000 to 7000
- materials: int32 [1024, 2048], P('tile'), may hold values from 0 to 7
- table: float32 [4, 8], replicated, may hold values from 0.2 to 5
- shifts: float32 [8], replicated, may hold values from 0.05 to 0.5
- shift_pick: int32 [1], replicated, may hold values from 0 to 7
Outputs:
- basis: float32 [64, 1024, 2048], P('fac', 'tile')
The draws below stay inside these ranges and needn't reach their ends.
All inputs are finite; a program needn't handle non-finite values.
Results may differ from the reference program's by a relative error of at most 0.0003.
Values sent between devices are 32-bit elements; how exact they have to be, the bound alone decides.
A program may use at most 64 MiB of HBM per device.

```python
import math
import jax
import jax.numpy as jnp
from jax import lax

COLS = 32
NZ = 64
SWEEPS = 4
NMAT = 8
NSHIFT = 8
NX = 1024
NYZ = 2048
NCOL = 64
NCELLS = 2097152


def draw_panel(key, part):
    keys = jax.random.split(key, 4)
    position = jnp.arange(NX, dtype=jnp.float32) / max(NX - 1, 1)
    row_scale = jnp.exp(jax.random.uniform(keys[1], (1, NX, 1), jnp.float32, 0.0, math.log(10.0)))
    base = jnp.clip(jax.random.normal(keys[0], (NCOL, NX, NYZ), jnp.float32), -4.0, 4.0)
    trend = jnp.exp(math.log(3.0) * position)
    column_scale = jnp.exp(jax.random.uniform(keys[3], (NCOL, 1, 1), jnp.float32, 0.0, math.log(10.0)))
    return base * column_scale * row_scale * trend[None, :, None]


def with_ends(entries, stream_key, low, high):
    place = [jax.random.randint(jax.random.fold_in(stream_key, axis), (), 0, length) for axis, length in enumerate(entries.shape)]
    longest = entries.shape.index(max(entries.shape))
    next_to = place[:longest] + [(place[longest] + 1) % entries.shape[longest]] + place[longest + 1:]
    return entries.at[tuple(place)].set(low).at[tuple(next_to)].set(high)


def setup_inputs(seed: int = 0) -> dict:
    key_of = jax.random.split(jax.random.key(seed), 6)
    panel = draw_panel(jax.random.fold_in(key_of[5], 71), 0)
    materials = with_ends(jax.random.randint(key_of[1], (NX, NYZ), 0, NMAT), jax.random.fold_in(key_of[1], 1), 0, NMAT - 1).astype(jnp.int32)
    table = jnp.clip(jnp.exp(jax.random.uniform(key_of[2], (4, NMAT), jnp.float32, math.log(0.2), math.log(5.0))), 0.2, 5.0)
    shifts = jnp.clip(jnp.exp(jax.random.uniform(key_of[3], (NSHIFT,), jnp.float32, math.log(0.05), math.log(0.5))), 0.05, 0.5)
    shift_pick = jax.random.randint(key_of[4], (1,), 0, NSHIFT).astype(jnp.int32)
    return dict(panel=panel, materials=materials, table=table, shifts=shifts, shift_pick=shift_pick)


OMEGA = 0.8

def harmonic(first, second):
    total = first + second
    safe = jnp.where(total > 0, total, 1.0)
    return 2.0 * first * second / safe

def material_fields(materials, table):
    fields = jnp.zeros((4,) + materials.shape, jnp.float32)
    for index in range(table.shape[1]):
        fields = fields + jnp.where(materials[None] == index, table[:, index][:, None, None], 0.0)
    return fields

def coefficients(fields, shift_value):
    cond_x = fields[0]
    faces_x = harmonic(cond_x[:-1], cond_x[1:])
    prev_x = faces_x[:-1]
    next_x = faces_x[1:]
    inner = fields[:, 1:-1]
    cond_y = inner[1]
    cond_z = inner[2]
    capacity = inner[3]
    count = cond_y.shape[0]
    width = cond_y.shape[1]
    zeros_y = jnp.zeros((count, NZ), jnp.float32)
    zeros_z = jnp.zeros((count, 1), jnp.float32)
    upper_y = jnp.concatenate([cond_y[:, NZ:], zeros_y], 1)
    next_y = harmonic(cond_y, upper_y)
    prev_y = jnp.concatenate([zeros_y, next_y[:, :-NZ]], 1)
    layer = jnp.arange(width) % NZ
    upper_z = jnp.concatenate([cond_z[:, 1:], zeros_z], 1)
    upper_z = jnp.where(layer[None] < NZ - 1, upper_z, 0.0)
    next_z = harmonic(cond_z, upper_z)
    prev_z = jnp.concatenate([zeros_z, next_z[:, :-1]], 1)
    diagonal = shift_value * capacity + prev_x + next_x + prev_y + next_y + prev_z + next_z
    inverse = jnp.where(capacity > 0, 1.0 / jnp.where(capacity > 0, diagonal, 1.0), 0.0)
    return (prev_x, next_x, prev_y, next_y, prev_z, next_z, inverse)

def relax(extended, source, coeffs):
    prev_x, next_x, prev_y, next_y, prev_z, next_z, inverse = coeffs
    center = extended[:, 1:-1]
    shape_y = center.shape[:-1] + (NZ,)
    shape_z = center.shape[:-1] + (1,)
    up_y = jnp.concatenate([center[..., NZ:], jnp.zeros(shape_y, center.dtype)], -1)
    down_y = jnp.concatenate([jnp.zeros(shape_y, center.dtype), center[..., :-NZ]], -1)
    up_z = jnp.concatenate([center[..., 1:], jnp.zeros(shape_z, center.dtype)], -1)
    down_z = jnp.concatenate([jnp.zeros(shape_z, center.dtype), center[..., :-1]], -1)
    beside = prev_x * extended[:, :-2] + next_x * extended[:, 2:]
    beside = beside + next_y * up_y + prev_y * down_y + next_z * up_z + prev_z * down_z
    return (1.0 - OMEGA) * center + OMEGA * (source + beside) * inverse

def reference(panel, materials, table, shifts, shift_pick):
    picker = jnp.arange(NSHIFT) == shift_pick[0]
    shift_value = jnp.sum(jnp.where(picker, shifts, 0.0))
    fields = material_fields(materials, table)
    padded = jnp.pad(fields, ((0, 0), (1, 1), (0, 0)))
    coeffs = coefficients(padded, shift_value)
    groups = panel.reshape(NCOL // 8, 8, NX, NYZ)

    def solve_group(source):
        values = source * coeffs[6][None]
        for sweep_index in range(SWEEPS):
            extended = jnp.pad(values, ((0, 0), (1, 1), (0, 0)))
            values = relax(extended, source, coeffs)
        return values
    solved = lax.map(solve_group, groups).reshape(NCOL, NX, NYZ)
    outputs = []
    for factor_id in range(2):
        matrix = solved[factor_id * COLS:(factor_id + 1) * COLS].reshape(COLS, NX * NYZ)
        gram = jnp.dot(matrix.astype(jnp.float32), matrix.T.astype(jnp.float32), precision=lax.Precision.HIGHEST, preferred_element_type=jnp.float32) / NCELLS
        lower_factor = jnp.linalg.cholesky(gram)
        ortho = lax.linalg.triangular_solve(lower_factor, matrix, left_side=True, lower=True)
        outputs.append(ortho.reshape(COLS, NX, NYZ))
    return jnp.concatenate(outputs, 0)
```

```python
import functools

import jax
import jax.numpy as jnp
from jax import lax
from jax.experimental import pallas as pl
from jax.experimental.pallas import tpu as pltpu
from jax.sharding import PartitionSpec as P

NZ = 64
SWEEPS = 4
OMEGA = 0.8
LANES = 128
YS = 4
CORES = 2
GROUP = 2 * YS * CORES
LINE = YS * CORES
HALO = 4
MESH = pl.DeviceIdType.MESH
HIGHEST = lax.Precision.HIGHEST


def chunked(value):
    return [value[:, i:i + LANES] for i in range(0, value.shape[1], LANES)]


def lane_iota(rows):
    return lax.broadcasted_iota(jnp.int32, (rows, LANES), 1)


def row_iota(rows):
    return lax.broadcasted_iota(jnp.int32, (rows, LANES), 0)


def pick_field(ids, table, field):
    low = (ids & 1) == 1
    mid = (ids & 2) == 2
    high = (ids & 4) == 4
    pairs = [jnp.where(low, table[field, i + 1], table[field, i]) for i in range(0, 8, 2)]
    quads = [jnp.where(mid, pairs[1], pairs[0]), jnp.where(mid, pairs[3], pairs[2])]
    return jnp.where(high, quads[1], quads[0])


def harmonic(first, second):
    return 2.0 * first * second / (first + second)


def make_coefficients(tiles, me, shift_value, ids_ref, table, coef, inv_ref):
    count = ids_ref.shape[1] // LANES
    ids = chunked(ids_ref[...])
    rows24 = row_iota(24)
    cut = ((me == 0) & (rows24 == 7)) | ((me == tiles - 1) & (rows24 == 15))
    lane = lane_iota(16)
    left = lane < NZ
    top = (lane % NZ) == NZ - 1
    cond_y = [pick_field(i[4:20], table, 1) for i in ids]
    turned = [pltpu.roll(v, NZ, 1) for v in cond_y]
    faces_y = []
    for k in range(count):
        above = jnp.where(left, turned[k], turned[min(k + 1, count - 1)])
        face = harmonic(cond_y[k], above)
        if k == count - 1:
            face = jnp.where(left, face, 0.0)
        faces_y.append(face)
    back_y = [pltpu.roll(v, NZ, 1) for v in faces_y]
    for k in range(count):
        below = back_y[k - 1] if k else jnp.zeros_like(back_y[0])
        next_y = faces_y[k]
        prev_y = jnp.where(left, below, back_y[k])
        cond_z = pick_field(ids[k][4:20], table, 2)
        next_z = harmonic(cond_z, pltpu.roll(cond_z, LANES - 1, 1))
        next_z = jnp.where(top, 0.0, next_z)
        prev_z = pltpu.roll(next_z, 1, 1)
        cond_x = pick_field(ids[k], table, 0)
        faces_x = harmonic(cond_x, pltpu.roll(cond_x, 23, 0))
        faces_x = jnp.where(cut, 0.0, faces_x)
        prev_x = faces_x[3:19]
        next_x = faces_x[4:20]
        capacity = pick_field(ids[k][4:20], table, 3)
        diagonal = shift_value * capacity + prev_x + next_x + prev_y + next_y + prev_z + next_z
        inverse = 1.0 / diagonal
        scaled = OMEGA * inverse
        where = pl.ds(k * LANES, LANES)
        for i, face in enumerate((prev_x, next_x, prev_y, next_y, prev_z, next_z)):
            coef[i, :, where] = face * scaled
        inv_ref[:, where] = inverse


def solve_column(source_ref, coef, inv_ref):
    count = inv_ref.shape[1] // LANES
    where = [pl.ds(k * LANES, LANES) for k in range(count)]
    left = lane_iota(16) < NZ
    values = [source_ref[:, where[k]] * inv_ref[:, where[k]] for k in range(count)]
    base = [OMEGA * v for v in values]
    for sweep in range(SWEEPS):
        turned = [pltpu.roll(v, NZ, 1) for v in values]
        new = []
        for k in range(count):
            v = values[k]
            total = (1.0 - OMEGA) * v + base[k]
            total += coef[0, :, where[k]] * pltpu.roll(v, 1, 0)
            total += coef[1, :, where[k]] * pltpu.roll(v, 15, 0)
            below = jnp.where(left, turned[max(k - 1, 0)], turned[k])
            above = jnp.where(left, turned[k], turned[min(k + 1, count - 1)])
            total += coef[2, :, where[k]] * below
            total += coef[3, :, where[k]] * above
            total += coef[4, :, where[k]] * pltpu.roll(v, 1, 1)
            total += coef[5, :, where[k]] * pltpu.roll(v, LANES - 1, 1)
            new.append(total)
        values = new
    return values


def diagonal_blocks(product):
    size = product.shape[0]
    keep = (row_iota(size) % 8) == (lane_iota(size) % 8)
    kept = jnp.where(keep, product, 0.0)
    return jnp.sum(kept.reshape(size // 8, 8, LANES), axis=1)


def pack(blocks):
    source = lax.broadcasted_iota(jnp.int32, (LANES, LANES), 0)
    target = lax.broadcasted_iota(jnp.int32, (LANES, LANES), 1)
    left, right = [], []
    for value, first_row, first_column in blocks:
        for half in range(2):
            left.append(value[half * 8:half * 8 + 8])
            place = (first_row + half * 8) * 4 + first_column + source // 8
            right.append((place == target).astype(jnp.float32))
    total = None
    for a, b in zip(left, right):
        part = jnp.dot(a, b, precision=HIGHEST, preferred_element_type=jnp.float32)
        total = part if total is None else total + part
    return total


def inverse_factor(packed, size):
    lane = lane_iota(8)
    eye_lane = lane_iota(size)
    eye_row = row_iota(size)
    tiles = [packed] + [pltpu.roll(packed, LANES - 32 * q, 1) for q in range(1, size // 8)]
    matrix = jnp.concatenate([jnp.where(lane < size, t, 0.0) for t in tiles], 0)
    matrix = jnp.where(eye_lane == eye_row + size, 1.0, matrix)
    for k in range(size - 1):
        row = matrix[k:k + 1, :]
        column = matrix[:, k:k + 1]
        pivot = 1.0 / matrix[k:k + 1, k:k + 1]
        factor = jnp.where(eye_row > k, column * pivot, 0.0)
        matrix = matrix - factor * row
    diagonal = jnp.sum(jnp.where(eye_lane == eye_row, matrix, 0.0), axis=1, keepdims=True)
    scaled = matrix * (1.0 / jnp.sqrt(diagonal))
    return pltpu.roll(scaled, LANES - size, 1)


def solve_kernel(tiles, panel, ids, table, shifts, pick, w_out, r_out, inv_out, ext, idx, coef, inv_ref, w, r, gbuf, zbuf,
                 ids_sem, own_sem, ids_send, ids_recv, halo_send, halo_recv, swap_send, swap_recv, rest_sem, out_sem,
                 group_send, group_recv, line_send, line_recv):
    cols = panel.shape[0]
    width = panel.shape[2]
    half = width // 2
    zs = tiles // LINE
    me = lax.axis_index("tile")
    fac = lax.axis_index("fac")
    parity = fac % 2
    partner = fac + 1 - 2 * parity
    line = me // LINE
    spot = me % LINE
    before = lax.rem(me + tiles - 1, tiles)
    after = lax.rem(me + 1, tiles)
    seat = parity * LINE + spot

    own_ids = pltpu.make_async_copy(ids, idx.at[pl.ds(8, 8)], ids_sem)
    own_ids.start()
    own_panel = pltpu.make_async_copy(panel, ext.at[:, pl.ds(HALO, 8)], own_sem)
    own_panel.start()

    def group_peer(step):
        there = lax.rem(seat + step, GROUP)
        peer_fac = fac - parity + there // LINE
        return {"tile": line * LINE + there % LINE, "fac": peer_fac}, there

    def line_peer(step):
        there = lax.rem(line + step, zs)
        return {"tile": there * LINE + spot, "fac": fac}, there

    barrier = pltpu.get_barrier_semaphore()
    greeted = [{"tile": before, "fac": fac}, {"tile": after, "fac": fac}]
    greeted += [group_peer(i)[0] for i in range(1, GROUP)]
    greeted += [line_peer(i)[0] for i in range(1, zs)]
    for peer in greeted:
        pl.semaphore_signal(barrier, inc=1, device_id=peer, device_id_type=MESH)
    pl.semaphore_wait(barrier, len(greeted))

    ids_up = pltpu.make_async_remote_copy(ids, idx.at[pl.ds(0, 8)], ids_send.at[0], ids_recv.at[0],
                                          device_id={"tile": after, "fac": fac}, device_id_type=MESH)
    ids_down = pltpu.make_async_remote_copy(ids, idx.at[pl.ds(16, 8)], ids_send.at[1], ids_recv.at[1],
                                            device_id={"tile": before, "fac": fac}, device_id_type=MESH)
    ids_up.start()
    ids_down.start()

    def halo_up(c):
        return pltpu.make_async_remote_copy(panel.at[c, pl.ds(8 - HALO, HALO)], ext.at[c, pl.ds(0, HALO)],
                                            halo_send.at[0, c], halo_recv.at[0, c],
                                            device_id={"tile": after, "fac": fac}, device_id_type=MESH)

    def halo_down(c):
        return pltpu.make_async_remote_copy(panel.at[c, pl.ds(0, HALO)], ext.at[c, pl.ds(8 + HALO, HALO)],
                                            halo_send.at[1, c], halo_recv.at[1, c],
                                            device_id={"tile": before, "fac": fac}, device_id_type=MESH)

    def send_halo(c, carry):
        halo_up(c).start()
        halo_down(c).start()
        return carry

    lax.fori_loop(0, cols, send_halo, 0)

    giving = pl.ds(pl.multiple_of(parity * half, half), half)
    getting = pl.ds(pl.multiple_of((1 - parity) * half, half), half)

    def swap(c):
        return pltpu.make_async_remote_copy(w.at[c, :, giving], r.at[c, :, giving], swap_send.at[c], swap_recv.at[c],
                                            device_id={"tile": me, "fac": partner}, device_id_type=MESH)

    shift_value = shifts[pick[0]]
    own_ids.wait()
    ids_up.wait()
    ids_down.wait()
    make_coefficients(tiles, me, shift_value, idx, table, coef, inv_ref)
    own_panel.wait()

    def column(c, carry):
        halo_up(c).wait()
        halo_down(c).wait()

        @pl.when(c > 0)
        def _():
            swap(c - 1).start()

        values = solve_column(ext.at[c], coef, inv_ref)
        for k, value in enumerate(values):
            w[c, :, pl.ds(k * LANES, LANES)] = value[HALO:HALO + 8]
        return carry

    lax.fori_loop(0, cols, column, 0)
    own = w[...].reshape(cols * 8, width)
    gram = lax.dot_general(own, own, (((1,), (1,)), ((), ())), precision=HIGHEST, preferred_element_type=jnp.float32)
    swap(cols - 1).start()
    own_blocks = diagonal_blocks(gram)
    keep_w = pltpu.make_async_copy(w, w_out, out_sem.at[0])
    keep_w.start()

    def arrived(c, carry):
        swap(c).wait()
        return carry

    lax.fori_loop(0, cols, arrived, 0)
    keep_r = pltpu.make_async_copy(r.at[:, :, getting], r_out.at[:, :, getting], out_sem.at[1])
    keep_r.start()
    mine = w[:, :, getting].reshape(cols * 8, half)
    theirs = r[:, :, getting].reshape(cols * 8, half)
    cross = lax.dot_general(mine, theirs, (((1,), (1,)), ((), ())), precision=HIGHEST, preferred_element_type=jnp.float32)
    across = lax.dot_general(theirs, mine, (((1,), (1,)), ((), ())), precision=HIGHEST, preferred_element_type=jnp.float32)
    mine_at = parity * cols
    theirs_at = cols - mine_at
    gbuf[seat] = pack([(own_blocks, mine_at, mine_at), (diagonal_blocks(cross), mine_at, theirs_at),
                       (diagonal_blocks(across), theirs_at, mine_at)])

    def group_copy(step):
        peer, _ = group_peer(step)
        return pltpu.make_async_remote_copy(gbuf.at[seat], gbuf.at[seat], group_send.at[step], group_recv.at[seat],
                                            device_id=peer, device_id_type=MESH)

    def group_arrival(step):
        peer, there = group_peer(step)
        return pltpu.make_async_remote_copy(gbuf.at[there], gbuf.at[there], group_send.at[step], group_recv.at[there],
                                            device_id=peer, device_id_type=MESH)

    def line_copy(step):
        peer, _ = line_peer(step)
        return pltpu.make_async_remote_copy(zbuf.at[line], zbuf.at[line], line_send.at[step], line_recv.at[line],
                                            device_id=peer, device_id_type=MESH)

    def line_arrival(step):
        peer, there = line_peer(step)
        return pltpu.make_async_remote_copy(zbuf.at[there], zbuf.at[there], line_send.at[step], line_recv.at[there],
                                            device_id=peer, device_id_type=MESH)

    rest = pltpu.make_async_remote_copy(w.at[:, :, pl.ds(half, half)], r_out.at[:, :, pl.ds(half, half)],
                                        rest_sem.at[0], rest_sem.at[1],
                                        device_id={"tile": me, "fac": partner}, device_id_type=MESH)
    for step in range(1, GROUP):
        group_copy(step).start()

    @pl.when(parity == 0)
    def _():
        rest.start()

    for step in range(1, GROUP):
        group_arrival(step).wait_recv()
    total = gbuf[0]
    for i in range(1, GROUP):
        total = total + gbuf[i]
    zbuf[line] = total
    order = sorted(range(1, zs), key=lambda s: -min(s, zs - s))
    for step in order:
        line_copy(step).start()
    for step in range(1, zs):
        line_arrival(step).wait_recv()
    total = zbuf[0]
    for i in range(1, zs):
        total = total + zbuf[i]
    cells = 8 * tiles * width
    inv_out[...] = inverse_factor(total / cells, 2 * cols)

    for step in range(1, GROUP):
        group_copy(step).wait_send()
    for step in range(1, zs):
        line_copy(step).wait_send()
    keep_w.wait()
    keep_r.wait()

    @pl.when(parity == 0)
    def _():
        rest.wait_send()

    @pl.when(parity == 1)
    def _():
        rest.wait_recv()


def split(value):
    high = value.astype(jnp.bfloat16)
    low = (value - high.astype(jnp.float32)).astype(jnp.bfloat16)
    return high, low


def dot3(a, b):
    ah, al = a
    bh, bl = b
    first = jnp.dot(ah, bh, preferred_element_type=jnp.float32)
    second = jnp.dot(ah, bl, preferred_element_type=jnp.float32)
    third = jnp.dot(al, bh, preferred_element_type=jnp.float32)
    return first + (second + third)


def apply_kernel(cols, inv, w, r, out, own_high, own_low, rec_high, rec_low):
    parity = lax.axis_index("fac") % 2

    @pl.when(pl.program_id(0) == 0)
    def _():
        rows = jnp.where(parity == 0, inv[0:cols, :], inv[cols:2 * cols, :])
        rows = jnp.broadcast_to(rows[:, None, :], (cols, 8, LANES)).reshape(cols * 8, LANES)
        high, low = split(rows)
        source = row_iota(LANES)
        target = lane_iota(LANES)
        same = (source % 8) == (target % 8)
        for first, ref_high, ref_low in ((parity * cols, own_high, own_low), (0, rec_high, rec_low)):
            spread = (source == first + target // 8).astype(jnp.bfloat16)
            for value, ref in ((high, ref_high), (low, ref_low)):
                wide = jnp.dot(value, spread, preferred_element_type=jnp.float32)
                ref[...] = jnp.where(same, wide, 0.0).astype(jnp.bfloat16)

    out[...] = dot3((own_high[...], own_low[...]), split(w[...]))

    @pl.when(parity == 1)
    def _():
        out[...] += dot3((rec_high[...], rec_low[...]), split(r[...]))


def per_device(tiles, panel, materials, table, shifts, shift_pick):
    cols, depth, width = panel.shape
    zs = tiles // LINE
    anywhere = pl.BlockSpec(memory_space=pl.ANY)
    scalars = pl.BlockSpec(memory_space=pltpu.SMEM)
    dma = pltpu.SemaphoreType.DMA
    f32 = jnp.float32
    w, r, inv = pl.pallas_call(
        functools.partial(solve_kernel, tiles),
        name="solve",
        out_shape=(jax.ShapeDtypeStruct((cols, depth, width), f32), jax.ShapeDtypeStruct((cols, depth, width), f32),
                   jax.ShapeDtypeStruct((2 * cols, LANES), f32)),
        in_specs=[anywhere, anywhere, scalars, scalars, scalars],
        out_specs=(anywhere, anywhere, pl.BlockSpec(memory_space=pltpu.VMEM)),
        scratch_shapes=[
            pltpu.VMEM((cols, 16, width), f32),
            pltpu.VMEM((24, width), jnp.int32),
            pltpu.VMEM((6, 16, width), f32),
            pltpu.VMEM((16, width), f32),
            pltpu.VMEM((cols, depth, width), f32),
            pltpu.VMEM((cols, depth, width), f32),
            pltpu.VMEM((GROUP, 8, LANES), f32),
            pltpu.VMEM((zs, 8, LANES), f32),
            dma, dma, dma((2,)), dma((2,)), dma((2, cols)), dma((2, cols)), dma((cols,)), dma((cols,)), dma((2,)), dma((2,)),
            dma((GROUP,)), dma((GROUP,)), dma((zs,)), dma((zs,)),
        ],
        compiler_params=pltpu.CompilerParams(collective_id=0, has_side_effects=True, vmem_limit_bytes=48 * 1024 * 1024),
    )(panel, materials, table, shifts, shift_pick)
    rows = cols * depth
    block = min(width, 512)
    tile = pl.BlockSpec((rows, block), lambda i: (0, i))
    basis = pl.pallas_call(
        functools.partial(apply_kernel, cols),
        name="apply",
        grid=(width // block,),
        out_shape=jax.ShapeDtypeStruct((rows, width), f32),
        in_specs=[pl.BlockSpec((2 * cols, LANES), lambda i: (0, 0)), tile, tile],
        out_specs=tile,
        scratch_shapes=[pltpu.VMEM((rows, LANES), jnp.bfloat16)] * 4,
    )(inv, w.reshape(rows, width), r.reshape(rows, width))
    return basis.reshape(cols, depth, width)


def solution(mesh):
    placed = (P("fac", "tile", None), P("tile", None), P(), P(), P())
    return jax.shard_map(
        functools.partial(per_device, mesh.shape["tile"]), mesh=mesh, in_specs=placed,
        out_specs=P("fac", "tile", None), check_vma=False,
    )
```

```python
import functools

import jax
import jax.numpy as jnp
from jax import lax
from jax.experimental import pallas as pl
from jax.experimental.pallas import tpu as pltpu
from jax.sharding import PartitionSpec as P

NZ = 64
SWEEPS = 4
OMEGA = 0.8
LANES = 128
YS = 4
CORES = 2
GROUP = 2 * YS * CORES
LINE = YS * CORES
HALO = 4
MESH = pl.DeviceIdType.MESH
HIGHEST = lax.Precision.HIGHEST


def chunked(value):
    return [value[:, i:i + LANES] for i in range(0, value.shape[1], LANES)]


def lane_iota(rows):
    return lax.broadcasted_iota(jnp.int32, (rows, LANES), 1)


def row_iota(rows):
    return lax.broadcasted_iota(jnp.int32, (rows, LANES), 0)


def pick_field(ids, table, field):
    low = (ids & 1) == 1
    mid = (ids & 2) == 2
    high = (ids & 4) == 4
    pairs = [jnp.where(low, table[field, i + 1], table[field, i]) for i in range(0, 8, 2)]
    quads = [jnp.where(mid, pairs[1], pairs[0]), jnp.where(mid, pairs[3], pairs[2])]
    return jnp.where(high, quads[1], quads[0])


def harmonic(first, second):
    return 2.0 * first * second / (first + second)


def make_coefficients(tiles, me, shift_value, ids_ref, table, coef, inv_ref):
    count = ids_ref.shape[1] // LANES
    ids = chunked(ids_ref[...])
    rows24 = row_iota(24)
    cut = ((me == 0) & (rows24 == 7)) | ((me == tiles - 1) & (rows24 == 15))
    lane = lane_iota(16)
    left = lane < NZ
    top = (lane % NZ) == NZ - 1
    cond_y = [pick_field(i[4:20], table, 1) for i in ids]
    turned = [pltpu.roll(v, NZ, 1) for v in cond_y]
    faces_y = []
    for k in range(count):
        above = jnp.where(left, turned[k], turned[min(k + 1, count - 1)])
        face = harmonic(cond_y[k], above)
        if k == count - 1:
            face = jnp.where(left, face, 0.0)
        faces_y.append(face)
    back_y = [pltpu.roll(v, NZ, 1) for v in faces_y]
    for k in range(count):
        below = back_y[k - 1] if k else jnp.zeros_like(back_y[0])
        next_y = faces_y[k]
        prev_y = jnp.where(left, below, back_y[k])
        cond_z = pick_field(ids[k][4:20], table, 2)
        next_z = harmonic(cond_z, pltpu.roll(cond_z, LANES - 1, 1))
        next_z = jnp.where(top, 0.0, next_z)
        prev_z = pltpu.roll(next_z, 1, 1)
        cond_x = pick_field(ids[k], table, 0)
        faces_x = harmonic(cond_x, pltpu.roll(cond_x, 23, 0))
        faces_x = jnp.where(cut, 0.0, faces_x)
        prev_x = faces_x[3:19]
        next_x = faces_x[4:20]
        capacity = pick_field(ids[k][4:20], table, 3)
        diagonal = shift_value * capacity + prev_x + next_x + prev_y + next_y + prev_z + next_z
        inverse = 1.0 / diagonal
        scaled = OMEGA * inverse
        where = pl.ds(k * LANES, LANES)
        for i, face in enumerate((prev_x, next_x, prev_y, next_y, prev_z, next_z)):
            coef[i, :, where] = face * scaled
        inv_ref[:, where] = inverse


def solve_column(source_ref, coef, inv_ref):
    count = inv_ref.shape[1] // LANES
    where = [pl.ds(k * LANES, LANES) for k in range(count)]
    left = lane_iota(16) < NZ
    values = [source_ref[:, where[k]] * inv_ref[:, where[k]] for k in range(count)]
    base = [OMEGA * v for v in values]
    for sweep in range(SWEEPS):
        turned = [pltpu.roll(v, NZ, 1) for v in values]
        new = []
        for k in range(count):
            v = values[k]
            total = (1.0 - OMEGA) * v + base[k]
            total += coef[0, :, where[k]] * pltpu.roll(v, 1, 0)
            total += coef[1, :, where[k]] * pltpu.roll(v, 15, 0)
            below = jnp.where(left, turned[max(k - 1, 0)], turned[k])
            above = jnp.where(left, turned[k], turned[min(k + 1, count - 1)])
            total += coef[2, :, where[k]] * below
            total += coef[3, :, where[k]] * above
            total += coef[4, :, where[k]] * pltpu.roll(v, 1, 1)
            total += coef[5, :, where[k]] * pltpu.roll(v, LANES - 1, 1)
            new.append(total)
        values = new
    return values


def diagonal_blocks(product):
    size = product.shape[0]
    keep = (row_iota(size) % 8) == (lane_iota(size) % 8)
    kept = jnp.where(keep, product, 0.0)
    return jnp.sum(kept.reshape(size // 8, 8, LANES), axis=1)


def pack(blocks):
    source = lax.broadcasted_iota(jnp.int32, (LANES, LANES), 0)
    target = lax.broadcasted_iota(jnp.int32, (LANES, LANES), 1)
    left, right = [], []
    for value, first_row, first_column in blocks:
        for half in range(2):
            left.append(value[half * 8:half * 8 + 8])
            place = (first_row + half * 8) * 4 + first_column + source // 8
            right.append((place == target).astype(jnp.float32))
    total = None
    for a, b in zip(left, right):
        part = jnp.dot(a, b, precision=HIGHEST, preferred_element_type=jnp.float32)
        total = part if total is None else total + part
    return total


def inverse_factor(packed, size):
    lane = lane_iota(8)
    eye_lane = lane_iota(size)
    eye_row = row_iota(size)
    tiles = [packed] + [pltpu.roll(packed, LANES - 32 * q, 1) for q in range(1, size // 8)]
    matrix = jnp.concatenate([jnp.where(lane < size, t, 0.0) for t in tiles], 0)
    matrix = jnp.where(eye_lane == eye_row + size, 1.0, matrix)
    for k in range(size - 1):
        row = matrix[k:k + 1, :]
        column = matrix[:, k:k + 1]
        pivot = 1.0 / matrix[k:k + 1, k:k + 1]
        factor = jnp.where(eye_row > k, column * pivot, 0.0)
        matrix = matrix - factor * row
    diagonal = jnp.sum(jnp.where(eye_lane == eye_row, matrix, 0.0), axis=1, keepdims=True)
    scaled = matrix * (1.0 / jnp.sqrt(diagonal))
    return pltpu.roll(scaled, LANES - size, 1)


def solve_kernel(tiles, panel, ids, table_hbm, shifts_hbm, pick, w, r, inv_out, table, shifts,
                 ext, idx, coef, inv_ref, gbuf, zbuf, token,
                 scalar_sem, ids_sem, own_sem, ids_send, ids_recv, halo_send, halo_recv, swap_send, swap_recv, rest_sem,
                 group_send, group_recv, line_send, line_recv):
    cols = panel.shape[0]
    width = panel.shape[2]
    half = width // 2
    zs = tiles // LINE
    me = lax.axis_index("tile")
    fac = lax.axis_index("fac")
    parity = fac % 2
    partner = fac + 1 - 2 * parity
    line = me // LINE
    spot = me % LINE
    before = lax.rem(me + tiles - 1, tiles)
    after = lax.rem(me + 1, tiles)
    seat = parity * LINE + spot

    scalars = [pltpu.make_async_copy(a, b, scalar_sem.at[i])
               for i, (a, b) in enumerate(((table_hbm, table), (shifts_hbm, shifts)))]
    own_ids = pltpu.make_async_copy(ids, idx.at[pl.ds(8, 8)], ids_sem)
    own_panel = pltpu.make_async_copy(panel, ext.at[:, pl.ds(HALO, 8)], own_sem)

    def group_peer(step):
        there = lax.rem(seat + step, GROUP)
        peer_fac = fac - parity + there // LINE
        return {"tile": line * LINE + there % LINE, "fac": peer_fac}, there

    def line_peer(step):
        there = lax.rem(line + step, zs)
        return {"tile": there * LINE + spot, "fac": fac}, there

    def along(distance):
        return {"tile": lax.rem(line + distance + zs, zs) * LINE + spot, "fac": fac}

    barrier = pltpu.get_barrier_semaphore()
    near = {"tile": me, "fac": partner}
    greeted = [{"tile": before, "fac": fac}, {"tile": after, "fac": fac}, near]
    greeted += [{"tile": line * LINE + lax.rem(spot + i, LINE), "fac": fac} for i in range(1, LINE)]
    greeted += [along(i) for i in (-2, -1, 1, 2)]
    for peer in greeted:
        pl.semaphore_signal(barrier, inc=1, device_id=peer, device_id_type=MESH)
    for copy in scalars + [own_ids, own_panel]:
        copy.start()
    pl.semaphore_wait(barrier, len(greeted))

    def greet(turn):
        pl.semaphore_signal(token.at[2 * turn], inc=1, device_id=along(2), device_id_type=MESH)
        pl.semaphore_signal(token.at[2 * turn + 1], inc=1, device_id=along(-2), device_id_type=MESH)

    def greeted_by(turn):
        pl.semaphore_wait(token.at[2 * turn], 1)
        pl.semaphore_wait(token.at[2 * turn + 1], 1)

    ids_up = pltpu.make_async_remote_copy(ids.at[pl.ds(3, 5)], idx.at[pl.ds(3, 5)], ids_send.at[0], ids_recv.at[0],
                                          device_id={"tile": after, "fac": fac}, device_id_type=MESH)
    ids_down = pltpu.make_async_remote_copy(ids.at[pl.ds(0, 5)], idx.at[pl.ds(16, 5)], ids_send.at[1], ids_recv.at[1],
                                            device_id={"tile": before, "fac": fac}, device_id_type=MESH)
    ids_up.start()
    ids_down.start()

    def halo_up(c):
        return pltpu.make_async_remote_copy(panel.at[c, pl.ds(8 - HALO, HALO)], ext.at[c, pl.ds(0, HALO)],
                                            halo_send.at[0, c], halo_recv.at[0, c],
                                            device_id={"tile": after, "fac": fac}, device_id_type=MESH)

    def halo_down(c):
        return pltpu.make_async_remote_copy(panel.at[c, pl.ds(0, HALO)], ext.at[c, pl.ds(8 + HALO, HALO)],
                                            halo_send.at[1, c], halo_recv.at[1, c],
                                            device_id={"tile": before, "fac": fac}, device_id_type=MESH)

    def send_halo(c, carry):
        halo_up(c).start()
        halo_down(c).start()
        return carry

    lax.fori_loop(0, cols, send_halo, 0)

    giving = pl.ds(pl.multiple_of(parity * half, half), half)
    getting = pl.ds(pl.multiple_of((1 - parity) * half, half), half)

    def swap(c):
        return pltpu.make_async_remote_copy(w.at[c, :, giving], r.at[c, :, giving], swap_send.at[c], swap_recv.at[c],
                                            device_id={"tile": me, "fac": partner}, device_id_type=MESH)

    pl.semaphore_signal(token.at[6], inc=1, device_id=near, device_id_type=MESH)
    greet(0)
    for copy in scalars:
        copy.wait()
    shift_value = shifts[pick[0]]
    own_ids.wait()
    ids_up.wait()
    ids_down.wait()
    make_coefficients(tiles, me, shift_value, idx, table, coef, inv_ref)
    own_panel.wait()

    def column(c, carry):
        halo_up(c).wait()
        halo_down(c).wait()

        @pl.when(c > 0)
        def _():
            swap(c - 1).start()

        for turn in range(3):
            @pl.when(c == 4 * (turn + 1))
            def _():
                greeted_by(turn)
                if turn < 2:
                    greet(turn + 1)

        values = solve_column(ext.at[c], coef, inv_ref)
        for k, value in enumerate(values):
            w[c, :, pl.ds(k * LANES, LANES)] = value[HALO:HALO + 8]
        return carry

    lax.fori_loop(0, cols, column, 0)
    own = w[...].reshape(cols * 8, width)
    gram = lax.dot_general(own, own, (((1,), (1,)), ((), ())), precision=HIGHEST, preferred_element_type=jnp.float32)
    swap(cols - 1).start()
    own_blocks = diagonal_blocks(gram)

    def arrived(c, carry):
        swap(c).wait()
        return carry

    lax.fori_loop(0, cols, arrived, 0)
    mine = w[:, :, getting].reshape(cols * 8, half)
    theirs = r[:, :, getting].reshape(cols * 8, half)
    cross = lax.dot_general(mine, theirs, (((1,), (1,)), ((), ())), precision=HIGHEST, preferred_element_type=jnp.float32)
    across = lax.dot_general(theirs, mine, (((1,), (1,)), ((), ())), precision=HIGHEST, preferred_element_type=jnp.float32)
    mine_at = parity * cols
    theirs_at = cols - mine_at
    gbuf[seat] = pack([(own_blocks, mine_at, mine_at), (diagonal_blocks(cross), mine_at, theirs_at),
                       (diagonal_blocks(across), theirs_at, mine_at)])

    def group_copy(step):
        peer, _ = group_peer(step)
        return pltpu.make_async_remote_copy(gbuf.at[seat], gbuf.at[seat], group_send.at[step], group_recv.at[seat],
                                            device_id=peer, device_id_type=MESH)

    def group_arrival(step):
        peer, there = group_peer(step)
        return pltpu.make_async_remote_copy(gbuf.at[there], gbuf.at[there], group_send.at[step], group_recv.at[there],
                                            device_id=peer, device_id_type=MESH)

    def line_copy(step):
        peer, _ = line_peer(step)
        return pltpu.make_async_remote_copy(zbuf.at[line], zbuf.at[line], line_send.at[step], line_recv.at[line],
                                            device_id=peer, device_id_type=MESH)

    def line_arrival(step):
        peer, there = line_peer(step)
        return pltpu.make_async_remote_copy(zbuf.at[there], zbuf.at[there], line_send.at[step], line_recv.at[there],
                                            device_id=peer, device_id_type=MESH)

    rest = pltpu.make_async_remote_copy(w.at[:, :, pl.ds(half, half)], r.at[:, :, pl.ds(half, half)],
                                        rest_sem.at[0], rest_sem.at[1],
                                        device_id={"tile": me, "fac": partner}, device_id_type=MESH)
    pl.semaphore_wait(token.at[6], 1)
    for step in range(1, GROUP):
        group_copy(step).start()

    @pl.when(parity == 0)
    def _():
        rest.start()

    for step in range(1, GROUP):
        group_arrival(step).wait_recv()
    total = gbuf[0]
    for i in range(1, GROUP):
        total = total + gbuf[i]
    zbuf[line] = total
    order = sorted(range(1, zs), key=lambda s: -min(s, zs - s))
    for step in order:
        line_copy(step).start()
    for step in range(1, zs):
        line_arrival(step).wait_recv()
    total = zbuf[0]
    for i in range(1, zs):
        total = total + zbuf[i]
    cells = 8 * tiles * width
    inv_out[...] = inverse_factor(total / cells, 2 * cols)

    for step in range(1, GROUP):
        group_copy(step).wait_send()
    for step in range(1, zs):
        line_copy(step).wait_send()

    @pl.when(parity == 0)
    def _():
        rest.wait_send()

    @pl.when(parity == 1)
    def _():
        rest.wait_recv()


def split(value):
    high = value.astype(jnp.bfloat16)
    low = (value - high.astype(jnp.float32)).astype(jnp.bfloat16)
    return high, low


def dot3(a, b):
    ah, al = a
    bh, bl = b
    first = jnp.dot(ah, bh, preferred_element_type=jnp.float32)
    second = jnp.dot(ah, bl, preferred_element_type=jnp.float32)
    third = jnp.dot(al, bh, preferred_element_type=jnp.float32)
    return first + (second + third)


def apply_kernel(cols, inv, w, r, out, stage, wide_high, wide_low, sems):
    parity = lax.axis_index("fac") % 2
    size = cols * 8
    width = w.shape[1]
    block = width // 4
    rows = jnp.where(parity == 0, inv[0:cols, :], inv[cols:2 * cols, :])
    rows = jnp.broadcast_to(rows[:, None, :], (cols, 8, LANES)).reshape(size, LANES)
    source = row_iota(LANES)
    target = lane_iota(LANES)
    same = (source % 8) == (target % 8)
    for value, ref in zip(split(rows), (wide_high, wide_low)):
        for part, first in ((0, parity * cols), (1, 0)):
            spread = (source == first + target // 8).astype(jnp.bfloat16)
            wide = jnp.dot(value, spread, preferred_element_type=jnp.float32)
            ref[:, part * size:(part + 1) * size] = jnp.where(same, wide, 0.0).astype(jnp.bfloat16)

    def send(k):
        part = pl.ds(k * block, block)
        return pltpu.make_async_copy(stage.at[:, part], out.at[:, part], sems.at[k])

    @pl.when(parity == 0)
    def _():
        for k in range(4):
            part = pl.ds(k * block, block)
            stage[:, part] = dot3((wide_high[:, 0:size], wide_low[:, 0:size]), split(w[:, part]))
            send(k).start()

    @pl.when(parity == 1)
    def _():
        for k in range(4):
            part = pl.ds(k * block, block)
            both = jnp.concatenate([w[:, part], r[:, part]], 0)
            stage[:, part] = dot3((wide_high[...], wide_low[...]), split(both))
            send(k).start()

    for k in range(4):
        send(k).wait()


def per_device(tiles, panel, materials, table, shifts, shift_pick):
    cols, depth, width = panel.shape
    zs = tiles // LINE
    hbm = pl.BlockSpec(memory_space=pltpu.HBM)
    vmem = pl.BlockSpec(memory_space=pltpu.VMEM)
    dma = pltpu.SemaphoreType.DMA
    f32 = jnp.float32
    w, r, inv = pl.pallas_call(
        functools.partial(solve_kernel, tiles),
        name="solve",
        out_shape=(jax.ShapeDtypeStruct((cols, depth, width), f32), jax.ShapeDtypeStruct((cols, depth, width), f32),
                   jax.ShapeDtypeStruct((2 * cols, LANES), f32)),
        in_specs=[hbm] * 4 + [pl.BlockSpec(memory_space=pltpu.SMEM)],
        out_specs=(vmem, vmem, vmem),
        scratch_shapes=[
            pltpu.SMEM(table.shape, f32),
            pltpu.SMEM(shifts.shape, f32),
            pltpu.VMEM((cols, 16, width), f32),
            pltpu.VMEM((24, width), jnp.int32),
            pltpu.VMEM((6, 16, width), f32),
            pltpu.VMEM((16, width), f32),
            pltpu.VMEM((GROUP, 8, LANES), f32),
            pltpu.VMEM((zs, 8, LANES), f32),
            pltpu.SemaphoreType.REGULAR((7,)),
            dma((2,)), dma, dma, dma((2,)), dma((2,)), dma((2, cols)), dma((2, cols)), dma((cols,)), dma((cols,)), dma((2,)),
            dma((GROUP,)), dma((GROUP,)), dma((zs,)), dma((zs,)),
        ],
        compiler_params=pltpu.CompilerParams(collective_id=0, has_side_effects=True, vmem_limit_bytes=32 * 1024 * 1024),
    )(*(pltpu.with_memory_space_constraint(a, pltpu.HBM) for a in (panel, materials, table, shifts)), shift_pick)
    rows = cols * depth
    basis = pl.pallas_call(
        functools.partial(apply_kernel, cols),
        name="apply",
        out_shape=jax.ShapeDtypeStruct((rows, width), f32),
        in_specs=[vmem] * 3,
        out_specs=hbm,
        scratch_shapes=[pltpu.VMEM((rows, width), f32), pltpu.VMEM((rows, 2 * rows), jnp.bfloat16),
                        pltpu.VMEM((rows, 2 * rows), jnp.bfloat16), dma((4,))],
        compiler_params=pltpu.CompilerParams(vmem_limit_bytes=32 * 1024 * 1024),
    )(inv, w.reshape(rows, width), r.reshape(rows, width))
    return basis.reshape(cols, depth, width)


def solution(mesh):
    placed = (P("fac", "tile", None), P("tile", None), P(), P(), P())
    return jax.shard_map(
        functools.partial(per_device, mesh.shape["tile"]), mesh=mesh, in_specs=placed,
        out_specs=P("fac", "tile", None), check_vma=False,
    )
```

```python
import functools

import jax
import jax.numpy as jnp
from jax import lax
from jax.experimental import pallas as pl
from jax.experimental.pallas import tpu as pltpu
from jax.sharding import PartitionSpec as P

NZ = 64
SWEEPS = 4
OMEGA = 0.8
LANES = 128
YS = 4
CORES = 2
GROUP = 2 * YS * CORES
LINE = YS * CORES
HALO = 4
MESH = pl.DeviceIdType.MESH
HIGHEST = lax.Precision.HIGHEST


def chunked(value):
    return [value[:, i:i + LANES] for i in range(0, value.shape[1], LANES)]


def lane_iota(rows):
    return lax.broadcasted_iota(jnp.int32, (rows, LANES), 1)


def row_iota(rows):
    return lax.broadcasted_iota(jnp.int32, (rows, LANES), 0)


def pick_field(ids, table, field):
    low = (ids & 1) == 1
    mid = (ids & 2) == 2
    high = (ids & 4) == 4
    pairs = [jnp.where(low, table[field, i + 1], table[field, i]) for i in range(0, 8, 2)]
    quads = [jnp.where(mid, pairs[1], pairs[0]), jnp.where(mid, pairs[3], pairs[2])]
    return jnp.where(high, quads[1], quads[0])


def harmonic(first, second):
    return 2.0 * first * second / (first + second)


def make_coefficients(tiles, me, shift_value, ids_ref, table, coef, inv_ref):
    count = ids_ref.shape[1] // LANES
    ids = chunked(ids_ref[...])
    rows24 = row_iota(24)
    cut = ((me == 0) & (rows24 == 7)) | ((me == tiles - 1) & (rows24 == 15))
    lane = lane_iota(16)
    left = lane < NZ
    top = (lane % NZ) == NZ - 1
    cond_y = [pick_field(i[4:20], table, 1) for i in ids]
    turned = [pltpu.roll(v, NZ, 1) for v in cond_y]
    faces_y = []
    for k in range(count):
        above = jnp.where(left, turned[k], turned[min(k + 1, count - 1)])
        face = harmonic(cond_y[k], above)
        if k == count - 1:
            face = jnp.where(left, face, 0.0)
        faces_y.append(face)
    back_y = [pltpu.roll(v, NZ, 1) for v in faces_y]
    for k in range(count):
        below = back_y[k - 1] if k else jnp.zeros_like(back_y[0])
        next_y = faces_y[k]
        prev_y = jnp.where(left, below, back_y[k])
        cond_z = pick_field(ids[k][4:20], table, 2)
        next_z = harmonic(cond_z, pltpu.roll(cond_z, LANES - 1, 1))
        next_z = jnp.where(top, 0.0, next_z)
        prev_z = pltpu.roll(next_z, 1, 1)
        cond_x = pick_field(ids[k], table, 0)
        faces_x = harmonic(cond_x, pltpu.roll(cond_x, 23, 0))
        faces_x = jnp.where(cut, 0.0, faces_x)
        prev_x = faces_x[3:19]
        next_x = faces_x[4:20]
        capacity = pick_field(ids[k][4:20], table, 3)
        diagonal = shift_value * capacity + prev_x + next_x + prev_y + next_y + prev_z + next_z
        inverse = 1.0 / diagonal
        scaled = OMEGA * inverse
        where = pl.ds(k * LANES, LANES)
        for i, face in enumerate((prev_x, next_x, prev_y, next_y, prev_z, next_z)):
            coef[i, :, where] = face * scaled
        inv_ref[:, where] = inverse


def solve_column(source_ref, coef, inv_ref):
    count = inv_ref.shape[1] // LANES
    where = [pl.ds(k * LANES, LANES) for k in range(count)]
    left = lane_iota(16) < NZ
    values = [source_ref[:, where[k]] * inv_ref[:, where[k]] for k in range(count)]
    base = [OMEGA * v for v in values]
    for sweep in range(SWEEPS):
        turned = [pltpu.roll(v, NZ, 1) for v in values]
        new = []
        for k in range(count):
            v = values[k]
            total = (1.0 - OMEGA) * v + base[k]
            total += coef[0, :, where[k]] * pltpu.roll(v, 1, 0)
            total += coef[1, :, where[k]] * pltpu.roll(v, 15, 0)
            below = jnp.where(left, turned[max(k - 1, 0)], turned[k])
            above = jnp.where(left, turned[k], turned[min(k + 1, count - 1)])
            total += coef[2, :, where[k]] * below
            total += coef[3, :, where[k]] * above
            total += coef[4, :, where[k]] * pltpu.roll(v, 1, 1)
            total += coef[5, :, where[k]] * pltpu.roll(v, LANES - 1, 1)
            new.append(total)
        values = new
    return values


def diagonal_blocks(product):
    size = product.shape[0]
    keep = (row_iota(size) % 8) == (lane_iota(size) % 8)
    kept = jnp.where(keep, product, 0.0)
    return jnp.sum(kept.reshape(size // 8, 8, LANES), axis=1)


def thirds(value):
    parts = []
    for _ in range(3):
        part = value.astype(jnp.bfloat16)
        parts.append(part)
        value = value - part.astype(jnp.float32)
    return jnp.concatenate(parts, 0)


def pack(value, first_row, first_column):
    source = lax.broadcasted_iota(jnp.int32, (LANES, LANES), 0)
    target = lax.broadcasted_iota(jnp.int32, (LANES, LANES), 1)
    places = []
    for half in range(2):
        place = (first_row + half * 8) * 4 + first_column + source // 8
        places.append((place == target).astype(jnp.bfloat16))
    left = jnp.concatenate([thirds(value[0:8]), thirds(value[8:16])], 1)
    found = jnp.dot(left, jnp.concatenate(places, 0), preferred_element_type=jnp.float32)
    return found[0:8] + (found[8:16] + found[16:24])


def inverse_factor(packed, size, out):
    count = size // 8
    row = row_iota(8)
    lane = lane_iota(8)

    def spread(value, r):
        return jnp.broadcast_to(value[r:r + 1, :], (8, LANES))

    left = {(j, q): jnp.broadcast_to(packed[:, 32 * q + j:32 * q + j + 1], (8, LANES))
            for j in range(size) for q in range(j // 8, count)}
    right = [jnp.where(lane == row + 8 * q, 1.0, 0.0) for q in range(count)]
    pivots = []
    for k in range(size):
        at, r = k // 8, k % 8
        pivot = 1.0 / spread(left[k, at], r)
        pivots.append(pivot)
        if k == size - 1:
            break
        scaled = {q: left[k, q] * pivot for q in range(at, count)}
        for j in range(k + 1, size):
            other = spread(scaled[j // 8], j % 8)
            for q in range(j // 8, count):
                left[j, q] = left[j, q] - left[k, q] * other
        source = spread(right[at], r)
        for q in range(at, count):
            factor = jnp.where(row > r, scaled[q], 0.0) if q == at else scaled[q]
            right[q] = right[q] - factor * source
    for q in range(count):
        scale = pivots[8 * q]
        for r in range(1, 8):
            scale = jnp.where(row == r, pivots[8 * q + r], scale)
        out[8 * q:8 * q + 8, :] = right[q] * jnp.sqrt(scale)


def solve_kernel(tiles, panel, ids, table_hbm, shifts_hbm, pick, w, r, inv_out, table, shifts,
                 ext, idx, coef, inv_ref, cross, gbuf, zbuf, token,
                 scalar_sem, ids_sem, own_sem, ids_send, ids_recv, halo_send, halo_recv, swap_send, swap_recv, rest_sem,
                 group_send, group_recv, line_send, line_recv):
    cols = panel.shape[0]
    width = panel.shape[2]
    half = width // 2
    zs = tiles // LINE
    me = lax.axis_index("tile")
    fac = lax.axis_index("fac")
    parity = fac % 2
    partner = fac + 1 - 2 * parity
    line = me // LINE
    spot = me % LINE
    before = lax.rem(me + tiles - 1, tiles)
    after = lax.rem(me + 1, tiles)
    seat = parity * LINE + spot

    scalars = [pltpu.make_async_copy(a, b, scalar_sem.at[i])
               for i, (a, b) in enumerate(((table_hbm, table), (shifts_hbm, shifts)))]
    own_ids = pltpu.make_async_copy(ids, idx.at[pl.ds(8, 8)], ids_sem)
    own_panel = pltpu.make_async_copy(panel, ext.at[:, pl.ds(HALO, 8)], own_sem)

    def group_peer(step):
        there = lax.rem(seat + step, GROUP)
        peer_fac = fac - parity + there // LINE
        return {"tile": line * LINE + there % LINE, "fac": peer_fac}, there

    def line_peer(step):
        there = lax.rem(line + step, zs)
        return {"tile": there * LINE + spot, "fac": fac}, there

    def along(distance):
        return {"tile": lax.rem(line + distance + zs, zs) * LINE + spot, "fac": fac}

    barrier = pltpu.get_barrier_semaphore()
    near = {"tile": me, "fac": partner}
    greeted = [{"tile": before, "fac": fac}, {"tile": after, "fac": fac}, near]
    greeted += [{"tile": line * LINE + lax.rem(spot + i, LINE), "fac": fac} for i in range(1, LINE)]
    greeted += [along(i) for i in (-2, -1, 1, 2)]
    for peer in greeted:
        pl.semaphore_signal(barrier, inc=1, device_id=peer, device_id_type=MESH)
    for copy in scalars + [own_ids, own_panel]:
        copy.start()
    pl.semaphore_wait(barrier, len(greeted))

    def greet(turn):
        pl.semaphore_signal(token.at[2 * turn], inc=1, device_id=along(2), device_id_type=MESH)
        pl.semaphore_signal(token.at[2 * turn + 1], inc=1, device_id=along(-2), device_id_type=MESH)

    def greeted_by(turn):
        pl.semaphore_wait(token.at[2 * turn], 1)
        pl.semaphore_wait(token.at[2 * turn + 1], 1)

    ids_up = pltpu.make_async_remote_copy(ids.at[pl.ds(3, 5)], idx.at[pl.ds(3, 5)], ids_send.at[0], ids_recv.at[0],
                                          device_id={"tile": after, "fac": fac}, device_id_type=MESH)
    ids_down = pltpu.make_async_remote_copy(ids.at[pl.ds(0, 5)], idx.at[pl.ds(16, 5)], ids_send.at[1], ids_recv.at[1],
                                            device_id={"tile": before, "fac": fac}, device_id_type=MESH)
    ids_up.start()
    ids_down.start()

    def halo_up(c):
        return pltpu.make_async_remote_copy(panel.at[c, pl.ds(8 - HALO, HALO)], ext.at[c, pl.ds(0, HALO)],
                                            halo_send.at[0, c], halo_recv.at[0, c],
                                            device_id={"tile": after, "fac": fac}, device_id_type=MESH)

    def halo_down(c):
        return pltpu.make_async_remote_copy(panel.at[c, pl.ds(0, HALO)], ext.at[c, pl.ds(8 + HALO, HALO)],
                                            halo_send.at[1, c], halo_recv.at[1, c],
                                            device_id={"tile": before, "fac": fac}, device_id_type=MESH)

    def send_halo(c, carry):
        halo_up(c).start()
        halo_down(c).start()
        return carry

    lax.fori_loop(0, cols, send_halo, 0)

    giving = pl.ds(pl.multiple_of(parity * half, half), half)
    getting = pl.ds(pl.multiple_of((1 - parity) * half, half), half)

    def swap(c):
        return pltpu.make_async_remote_copy(w.at[c, :, giving], r.at[c, :, giving], swap_send.at[c], swap_recv.at[c],
                                            device_id={"tile": me, "fac": partner}, device_id_type=MESH)

    pl.semaphore_signal(token.at[6], inc=1, device_id=near, device_id_type=MESH)
    greet(0)
    for copy in scalars:
        copy.wait()
    shift_value = shifts[pick[0]]
    own_ids.wait()
    ids_up.wait()
    ids_down.wait()
    make_coefficients(tiles, me, shift_value, idx, table, coef, inv_ref)
    own_panel.wait()

    def column(c, carry):
        halo_up(c).wait()
        halo_down(c).wait()

        @pl.when(c > 0)
        def _():
            swap(c - 1).start()

        for turn in range(3):
            @pl.when(c == 4 * (turn + 1))
            def _():
                greeted_by(turn)
                if turn < 2:
                    greet(turn + 1)

        values = solve_column(ext.at[c], coef, inv_ref)
        for k, value in enumerate(values):
            w[c, :, pl.ds(k * LANES, LANES)] = value[HALO:HALO + 8]
        return carry

    lax.fori_loop(0, cols, column, 0)
    own = w[...].reshape(cols * 8, width)
    gram = lax.dot_general(own, own, (((1,), (1,)), ((), ())), precision=HIGHEST, preferred_element_type=jnp.float32)
    swap(cols - 1).start()
    own_packed = pack(diagonal_blocks(gram), parity * cols, parity * cols)

    def arrived(c, carry):
        swap(c).wait()
        return carry

    lax.fori_loop(0, cols, arrived, 0)
    mine = w[:, :, getting].reshape(cols * 8, half)
    theirs = r[:, :, getting].reshape(cols * 8, half)

    def product(a, b):
        return lax.dot_general(a, b, (((1,), (1,)), ((), ())), precision=HIGHEST, preferred_element_type=jnp.float32)

    @pl.when(parity == 0)
    def _():
        cross[...] = product(theirs, mine)

    @pl.when(parity == 1)
    def _():
        cross[...] = product(mine, theirs)

    gbuf[seat] = own_packed + pack(diagonal_blocks(cross[...]), cols, 0)

    def group_copy(step):
        peer, _ = group_peer(step)
        return pltpu.make_async_remote_copy(gbuf.at[seat], gbuf.at[seat], group_send.at[step], group_recv.at[seat],
                                            device_id=peer, device_id_type=MESH)

    def group_arrival(step):
        peer, there = group_peer(step)
        return pltpu.make_async_remote_copy(gbuf.at[there], gbuf.at[there], group_send.at[step], group_recv.at[there],
                                            device_id=peer, device_id_type=MESH)

    def line_copy(step):
        peer, _ = line_peer(step)
        return pltpu.make_async_remote_copy(zbuf.at[line], zbuf.at[line], line_send.at[step], line_recv.at[line],
                                            device_id=peer, device_id_type=MESH)

    def line_arrival(step):
        peer, there = line_peer(step)
        return pltpu.make_async_remote_copy(zbuf.at[there], zbuf.at[there], line_send.at[step], line_recv.at[there],
                                            device_id=peer, device_id_type=MESH)

    rest = pltpu.make_async_remote_copy(w.at[:, :, pl.ds(half, half)], r.at[:, :, pl.ds(half, half)],
                                        rest_sem.at[0], rest_sem.at[1],
                                        device_id={"tile": me, "fac": partner}, device_id_type=MESH)
    pl.semaphore_wait(token.at[6], 1)
    for step in range(1, GROUP):
        group_copy(step).start()

    @pl.when(parity == 0)
    def _():
        rest.start()

    for step in range(1, GROUP):
        group_arrival(step).wait_recv()
    total = gbuf[0]
    for i in range(1, GROUP):
        total = total + gbuf[i]
    zbuf[line] = total
    order = sorted(range(1, zs), key=lambda s: -min(s, zs - s))
    for step in order:
        line_copy(step).start()
    for step in range(1, zs):
        line_arrival(step).wait_recv()
    total = zbuf[0]
    for i in range(1, zs):
        total = total + zbuf[i]
    cells = 8 * tiles * width
    inverse_factor(total / cells, 2 * cols, inv_out)

    for step in range(1, GROUP):
        group_copy(step).wait_send()
    for step in range(1, zs):
        line_copy(step).wait_send()

    @pl.when(parity == 0)
    def _():
        rest.wait_send()

    @pl.when(parity == 1)
    def _():
        rest.wait_recv()


def split(value):
    high = value.astype(jnp.bfloat16)
    low = (value - high.astype(jnp.float32)).astype(jnp.bfloat16)
    return high, low


def dot3(a, b):
    size = a.shape[0] // 2
    high, low = split(b)
    both = jnp.dot(a, high, preferred_element_type=jnp.float32)
    rest = jnp.dot(a[0:size], low, preferred_element_type=jnp.float32)
    return both[0:size] + (both[size:2 * size] + rest)


def apply_kernel(cols, inv, w, r, out, stage, factor, sems):
    parity = lax.axis_index("fac") % 2
    size = cols * 8
    width = w.shape[1]
    block = width // 4
    rows = jnp.where(parity == 0, inv[0:cols, :], inv[cols:2 * cols, :])
    rows = jnp.broadcast_to(rows[:, None, :], (cols, 8, LANES)).reshape(size, LANES)
    source = row_iota(LANES)
    target = lane_iota(LANES)
    same = (source % 8) == (target % 8)
    rows = jnp.concatenate(split(rows), 0)
    same = jnp.concatenate([same, same], 0)
    for part, first in ((0, parity * cols), (1, 0)):
        spread = (source == first + target // 8).astype(jnp.bfloat16)
        wide = jnp.dot(rows, spread, preferred_element_type=jnp.float32)
        factor[:, part * size:(part + 1) * size] = jnp.where(same, wide, 0.0).astype(jnp.bfloat16)

    def send(k):
        part = pl.ds(k * block, block)
        return pltpu.make_async_copy(stage.at[:, part], out.at[:, part], sems.at[k])

    @pl.when(parity == 0)
    def _():
        for k in range(4):
            part = pl.ds(k * block, block)
            stage[:, part] = dot3(factor[:, 0:size], w[:, part])
            send(k).start()

    @pl.when(parity == 1)
    def _():
        for k in range(4):
            part = pl.ds(k * block, block)
            both = jnp.concatenate([w[:, part], r[:, part]], 0)
            stage[:, part] = dot3(factor[...], both)
            send(k).start()

    for k in range(4):
        send(k).wait()


def per_device(tiles, panel, materials, table, shifts, shift_pick):
    cols, depth, width = panel.shape
    zs = tiles // LINE
    hbm = pl.BlockSpec(memory_space=pltpu.HBM)
    vmem = pl.BlockSpec(memory_space=pltpu.VMEM)
    dma = pltpu.SemaphoreType.DMA
    f32 = jnp.float32
    w, r, inv = pl.pallas_call(
        functools.partial(solve_kernel, tiles),
        name="solve",
        out_shape=(jax.ShapeDtypeStruct((cols, depth, width), f32), jax.ShapeDtypeStruct((cols, depth, width), f32),
                   jax.ShapeDtypeStruct((2 * cols, LANES), f32)),
        in_specs=[hbm] * 4 + [pl.BlockSpec(memory_space=pltpu.SMEM)],
        out_specs=(vmem, vmem, vmem),
        scratch_shapes=[
            pltpu.SMEM(table.shape, f32),
            pltpu.SMEM(shifts.shape, f32),
            pltpu.VMEM((cols, 16, width), f32),
            pltpu.VMEM((24, width), jnp.int32),
            pltpu.VMEM((6, 16, width), f32),
            pltpu.VMEM((16, width), f32),
            pltpu.VMEM((cols * depth, LANES), f32),
            pltpu.VMEM((GROUP, 8, LANES), f32),
            pltpu.VMEM((zs, 8, LANES), f32),
            pltpu.SemaphoreType.REGULAR((7,)),
            dma((2,)), dma, dma, dma((2,)), dma((2,)), dma((2, cols)), dma((2, cols)), dma((cols,)), dma((cols,)), dma((2,)),
            dma((GROUP,)), dma((GROUP,)), dma((zs,)), dma((zs,)),
        ],
        compiler_params=pltpu.CompilerParams(collective_id=0, has_side_effects=True, vmem_limit_bytes=32 * 1024 * 1024),
    )(*(pltpu.with_memory_space_constraint(a, pltpu.HBM) for a in (panel, materials, table, shifts)), shift_pick)
    rows = cols * depth
    basis = pl.pallas_call(
        functools.partial(apply_kernel, cols),
        name="apply",
        out_shape=jax.ShapeDtypeStruct((rows, width), f32),
        in_specs=[vmem] * 3,
        out_specs=hbm,
        scratch_shapes=[pltpu.VMEM((rows, width), f32), pltpu.VMEM((2 * rows, 2 * rows), jnp.bfloat16), dma((4,))],
        compiler_params=pltpu.CompilerParams(vmem_limit_bytes=32 * 1024 * 1024),
    )(inv, w.reshape(rows, width), r.reshape(rows, width))
    return basis.reshape(cols, depth, width)


def solution(mesh):
    placed = (P("fac", "tile", None), P("tile", None), P(), P(), P())
    return jax.shard_map(
        functools.partial(per_device, mesh.shape["tile"]), mesh=mesh, in_specs=placed,
        out_specs=P("fac", "tile", None), check_vma=False,
    )
```

```python
import functools

import jax
import jax.numpy as jnp
from jax import lax
from jax.experimental import pallas as pl
from jax.experimental.pallas import tpu as pltpu
from jax.sharding import PartitionSpec as P

NZ = 64
SWEEPS = 4
OMEGA = 0.8
LANES = 128
YS = 4
CORES = 2
GROUP = 2 * YS * CORES
LINE = YS * CORES
HALO = 4
MESH = pl.DeviceIdType.MESH
HIGHEST = lax.Precision.HIGHEST


def chunked(value):
    return [value[:, i:i + LANES] for i in range(0, value.shape[1], LANES)]


def lane_iota(rows):
    return lax.broadcasted_iota(jnp.int32, (rows, LANES), 1)


def row_iota(rows):
    return lax.broadcasted_iota(jnp.int32, (rows, LANES), 0)


def pick_field(ids, table, field):
    low = (ids & 1) == 1
    mid = (ids & 2) == 2
    high = (ids & 4) == 4
    pairs = [jnp.where(low, table[field, i + 1], table[field, i]) for i in range(0, 8, 2)]
    quads = [jnp.where(mid, pairs[1], pairs[0]), jnp.where(mid, pairs[3], pairs[2])]
    return jnp.where(high, quads[1], quads[0])


def harmonic(first, second):
    return 2.0 * first * second / (first + second)


def make_coefficients(tiles, me, shift_value, ids_ref, table, coef, inv_ref):
    count = ids_ref.shape[1] // LANES
    ids = chunked(ids_ref[...])
    rows24 = row_iota(24)
    cut = ((me == 0) & (rows24 == 7)) | ((me == tiles - 1) & (rows24 == 15))
    lane = lane_iota(16)
    left = lane < NZ
    top = (lane % NZ) == NZ - 1
    cond_y = [pick_field(i[4:20], table, 1) for i in ids]
    turned = [pltpu.roll(v, NZ, 1) for v in cond_y]
    faces_y = []
    for k in range(count):
        above = jnp.where(left, turned[k], turned[min(k + 1, count - 1)])
        face = harmonic(cond_y[k], above)
        if k == count - 1:
            face = jnp.where(left, face, 0.0)
        faces_y.append(face)
    back_y = [pltpu.roll(v, NZ, 1) for v in faces_y]
    for k in range(count):
        below = back_y[k - 1] if k else jnp.zeros_like(back_y[0])
        next_y = faces_y[k]
        prev_y = jnp.where(left, below, back_y[k])
        cond_z = pick_field(ids[k][4:20], table, 2)
        next_z = harmonic(cond_z, pltpu.roll(cond_z, LANES - 1, 1))
        next_z = jnp.where(top, 0.0, next_z)
        prev_z = pltpu.roll(next_z, 1, 1)
        cond_x = pick_field(ids[k], table, 0)
        faces_x = harmonic(cond_x, pltpu.roll(cond_x, 23, 0))
        faces_x = jnp.where(cut, 0.0, faces_x)
        prev_x = faces_x[3:19]
        next_x = faces_x[4:20]
        capacity = pick_field(ids[k][4:20], table, 3)
        diagonal = shift_value * capacity + prev_x + next_x + prev_y + next_y + prev_z + next_z
        inverse = 1.0 / diagonal
        scaled = OMEGA * inverse
        where = pl.ds(k * LANES, LANES)
        for i, face in enumerate((prev_x, next_x, prev_y, next_y, prev_z, next_z)):
            coef[i, :, where] = face * scaled
        inv_ref[:, where] = inverse


def solve_column(source_ref, coef, inv_ref):
    count = inv_ref.shape[1] // LANES
    where = [pl.ds(k * LANES, LANES) for k in range(count)]
    left = lane_iota(16) < NZ
    values = [source_ref[:, where[k]] * inv_ref[:, where[k]] for k in range(count)]
    base = [OMEGA * v for v in values]
    for sweep in range(SWEEPS):
        turned = [pltpu.roll(v, NZ, 1) for v in values]
        new = []
        for k in range(count):
            v = values[k]
            total = (1.0 - OMEGA) * v + base[k]
            total += coef[0, :, where[k]] * pltpu.roll(v, 1, 0)
            total += coef[1, :, where[k]] * pltpu.roll(v, 15, 0)
            below = jnp.where(left, turned[max(k - 1, 0)], turned[k])
            above = jnp.where(left, turned[k], turned[min(k + 1, count - 1)])
            total += coef[2, :, where[k]] * below
            total += coef[3, :, where[k]] * above
            total += coef[4, :, where[k]] * pltpu.roll(v, 1, 1)
            total += coef[5, :, where[k]] * pltpu.roll(v, LANES - 1, 1)
            new.append(total)
        values = new
    return values


def diagonal_blocks(product):
    size = product.shape[0]
    keep = (row_iota(size) % 8) == (lane_iota(size) % 8)
    kept = jnp.where(keep, product, 0.0)
    return jnp.sum(kept.reshape(size // 8, 8, LANES), axis=1)


def thirds(value):
    parts = []
    for _ in range(3):
        part = value.astype(jnp.bfloat16)
        parts.append(part)
        value = value - part.astype(jnp.float32)
    return jnp.concatenate(parts, 0)


def pack(value, first_row, first_column):
    source = lax.broadcasted_iota(jnp.int32, (LANES, LANES), 0)
    target = lax.broadcasted_iota(jnp.int32, (LANES, LANES), 1)
    places = []
    for half in range(2):
        place = (first_row + half * 8) * 4 + first_column + source // 8
        places.append((place == target).astype(jnp.bfloat16))
    left = jnp.concatenate([thirds(value[0:8]), thirds(value[8:16])], 1)
    found = jnp.dot(left, jnp.concatenate(places, 0), preferred_element_type=jnp.float32)
    return found[0:8] + (found[8:16] + found[16:24])


def inverse_factor(packed, size, out):
    count = size // 8
    row = row_iota(8)
    lane = lane_iota(8)

    def spread(value, r):
        return jnp.broadcast_to(value[r:r + 1, :], (8, LANES))

    left = {(j, q): jnp.broadcast_to(packed[:, 32 * q + j:32 * q + j + 1], (8, LANES))
            for j in range(size) for q in range(j // 8, count)}
    right = [jnp.where(lane == row + 8 * q, 1.0, 0.0) for q in range(count)]
    pivots = []
    for k in range(size):
        at, r = k // 8, k % 8
        pivot = 1.0 / spread(left[k, at], r)
        pivots.append(pivot)
        if k == size - 1:
            break
        scaled = {q: left[k, q] * pivot for q in range(at, count)}
        for j in range(k + 1, size):
            other = spread(scaled[j // 8], j % 8)
            for q in range(j // 8, count):
                left[j, q] = left[j, q] - left[k, q] * other
        source = spread(right[at], r)
        for q in range(at, count):
            factor = jnp.where(row > r, scaled[q], 0.0) if q == at else scaled[q]
            right[q] = right[q] - factor * source
    for q in range(count):
        scale = pivots[8 * q]
        for r in range(1, 8):
            scale = jnp.where(row == r, pivots[8 * q + r], scale)
        out[8 * q:8 * q + 8, :] = right[q] * jnp.sqrt(scale)


def solve_kernel(tiles, panel, ids, table_hbm, shifts_hbm, pick, w, r, inv_out, table, shifts,
                 ext, idx, coef, inv_ref, cross, gbuf, zbuf, token,
                 scalar_sem, ids_sem, own_sem, ids_send, ids_recv, halo_send, halo_recv, swap_send, swap_recv, rest_send, rest_recv,
                 group_send, group_recv, line_send, line_recv):
    cols = panel.shape[0]
    width = panel.shape[2]
    half = width // 2
    zs = tiles // LINE
    me = lax.axis_index("tile")
    fac = lax.axis_index("fac")
    parity = fac % 2
    partner = fac + 1 - 2 * parity
    line = me // LINE
    spot = me % LINE
    before = lax.rem(me + tiles - 1, tiles)
    after = lax.rem(me + 1, tiles)
    seat = parity * LINE + spot

    scalars = [pltpu.make_async_copy(a, b, scalar_sem.at[i])
               for i, (a, b) in enumerate(((table_hbm, table), (shifts_hbm, shifts)))]
    own_ids = pltpu.make_async_copy(ids, idx.at[pl.ds(8, 8)], ids_sem)
    own_panel = pltpu.make_async_copy(panel, ext.at[:, pl.ds(HALO, 8)], own_sem)

    def group_peer(step):
        there = lax.rem(seat + step, GROUP)
        peer_fac = fac - parity + there // LINE
        return {"tile": line * LINE + there % LINE, "fac": peer_fac}, there

    def line_peer(step):
        there = lax.rem(line + step, zs)
        return {"tile": there * LINE + spot, "fac": fac}, there

    def along(distance):
        return {"tile": lax.rem(line + distance + zs, zs) * LINE + spot, "fac": fac}

    barrier = pltpu.get_barrier_semaphore()
    near = {"tile": me, "fac": partner}
    greeted = [{"tile": before, "fac": fac}, {"tile": after, "fac": fac}, near]
    greeted += [{"tile": line * LINE + lax.rem(spot + i, LINE), "fac": fac} for i in range(1, LINE)]
    greeted += [along(i) for i in (-2, -1, 1, 2)]
    for peer in greeted:
        pl.semaphore_signal(barrier, inc=1, device_id=peer, device_id_type=MESH)
    for copy in scalars + [own_ids, own_panel]:
        copy.start()
    pl.semaphore_wait(barrier, len(greeted))

    def greet(turn):
        pl.semaphore_signal(token.at[2 * turn], inc=1, device_id=along(2), device_id_type=MESH)
        pl.semaphore_signal(token.at[2 * turn + 1], inc=1, device_id=along(-2), device_id_type=MESH)

    def greeted_by(turn):
        pl.semaphore_wait(token.at[2 * turn], 1)
        pl.semaphore_wait(token.at[2 * turn + 1], 1)

    ids_up = pltpu.make_async_remote_copy(ids.at[pl.ds(3, 5)], idx.at[pl.ds(3, 5)], ids_send.at[0], ids_recv.at[0],
                                          device_id={"tile": after, "fac": fac}, device_id_type=MESH)
    ids_down = pltpu.make_async_remote_copy(ids.at[pl.ds(0, 5)], idx.at[pl.ds(16, 5)], ids_send.at[1], ids_recv.at[1],
                                            device_id={"tile": before, "fac": fac}, device_id_type=MESH)
    ids_up.start()
    ids_down.start()

    def halo_up(c):
        return pltpu.make_async_remote_copy(panel.at[c, pl.ds(8 - HALO, HALO)], ext.at[c, pl.ds(0, HALO)],
                                            halo_send.at[0, c], halo_recv.at[0, c],
                                            device_id={"tile": after, "fac": fac}, device_id_type=MESH)

    def halo_down(c):
        return pltpu.make_async_remote_copy(panel.at[c, pl.ds(0, HALO)], ext.at[c, pl.ds(8 + HALO, HALO)],
                                            halo_send.at[1, c], halo_recv.at[1, c],
                                            device_id={"tile": before, "fac": fac}, device_id_type=MESH)

    def send_halo(c, carry):
        halo_up(c).start()
        halo_down(c).start()
        return carry

    lax.fori_loop(0, cols, send_halo, 0)

    giving = pl.ds(pl.multiple_of(parity * half, half), half)

    def swap(c):
        return pltpu.make_async_remote_copy(w.at[c, :, giving], r.at[c, :, giving], swap_send.at[c], swap_recv.at[c],
                                            device_id={"tile": me, "fac": partner}, device_id_type=MESH)

    pl.semaphore_signal(token.at[6], inc=1, device_id=near, device_id_type=MESH)
    greet(0)
    for copy in scalars:
        copy.wait()
    shift_value = shifts[pick[0]]
    own_ids.wait()
    ids_up.wait()
    ids_down.wait()
    make_coefficients(tiles, me, shift_value, idx, table, coef, inv_ref)
    own_panel.wait()

    def column(c, carry):
        halo_up(c).wait()
        halo_down(c).wait()

        @pl.when(c > 0)
        def _():
            swap(c - 1).start()

        for turn in range(3):
            @pl.when(c == 4 * (turn + 1))
            def _():
                greeted_by(turn)
                if turn < 2:
                    greet(turn + 1)

        values = solve_column(ext.at[c], coef, inv_ref)
        for k, value in enumerate(values):
            w[c, :, pl.ds(k * LANES, LANES)] = value[HALO:HALO + 8]
        return carry

    lax.fori_loop(0, cols, column, 0)
    def rest(part):
        some = pl.ds(0, cols // 4) if part == 0 else pl.ds(cols // 4, cols - cols // 4)
        side = pl.ds(half, half)
        return pltpu.make_async_remote_copy(w.at[some, :, side], r.at[some, :, side], rest_send.at[part], rest_recv.at[part],
                                            device_id=near, device_id_type=MESH)

    own = w[...].reshape(cols * 8, width)
    gram = lax.dot_general(own, own, (((1,), (1,)), ((), ())), precision=HIGHEST, preferred_element_type=jnp.float32)
    swap(cols - 1).start()

    @pl.when(parity == 0)
    def _():
        rest(0).start()

    own_packed = pack(diagonal_blocks(gram), parity * cols, parity * cols)

    def arrived(c, carry):
        swap(c).wait()
        return carry

    def product(a, b):
        return lax.dot_general(a, b, (((1,), (1,)), ((), ())), precision=HIGHEST, preferred_element_type=jnp.float32)

    early = cols - cols // 4
    for first, last in ((0, early), (early, cols)):
        lax.fori_loop(first, last, arrived, 0)

        @pl.when(parity == 0)
        def _():
            mine = w[:, :, half:].reshape(cols * 8, half)
            cross[8 * first:8 * last, :] = product(r[first:last, :, half:].reshape((last - first) * 8, half), mine)

        @pl.when(parity == 1)
        def _():
            mine = w[:, :, 0:half].reshape(cols * 8, half)
            cross[:, 8 * first:8 * last] = product(mine, r[first:last, :, 0:half].reshape((last - first) * 8, half))

    gbuf[seat] = own_packed + pack(diagonal_blocks(cross[...]), cols, 0)

    def group_copy(step):
        peer, _ = group_peer(step)
        return pltpu.make_async_remote_copy(gbuf.at[seat], gbuf.at[seat], group_send.at[step], group_recv.at[seat],
                                            device_id=peer, device_id_type=MESH)

    def group_arrival(step):
        peer, there = group_peer(step)
        return pltpu.make_async_remote_copy(gbuf.at[there], gbuf.at[there], group_send.at[step], group_recv.at[there],
                                            device_id=peer, device_id_type=MESH)

    def line_copy(step):
        peer, _ = line_peer(step)
        return pltpu.make_async_remote_copy(zbuf.at[line], zbuf.at[line], line_send.at[step], line_recv.at[line],
                                            device_id=peer, device_id_type=MESH)

    def line_arrival(step):
        peer, there = line_peer(step)
        return pltpu.make_async_remote_copy(zbuf.at[there], zbuf.at[there], line_send.at[step], line_recv.at[there],
                                            device_id=peer, device_id_type=MESH)

    pl.semaphore_wait(token.at[6], 1)
    for step in range(1, GROUP):
        group_copy(step).start()

    @pl.when(parity == 0)
    def _():
        rest(1).start()

    for step in range(1, GROUP):
        group_arrival(step).wait_recv()
    total = gbuf[0]
    for i in range(1, GROUP):
        total = total + gbuf[i]
    zbuf[line] = total
    order = sorted(range(1, zs), key=lambda s: -min(s, zs - s))
    for step in order:
        line_copy(step).start()
    for step in range(1, zs):
        line_arrival(step).wait_recv()
    total = zbuf[0]
    for i in range(1, zs):
        total = total + zbuf[i]
    cells = 8 * tiles * width
    inverse_factor(total / cells, 2 * cols, inv_out)

    for step in range(1, GROUP):
        group_copy(step).wait_send()
    for step in range(1, zs):
        line_copy(step).wait_send()

    @pl.when(parity == 0)
    def _():
        rest(0).wait_send()
        rest(1).wait_send()

    @pl.when(parity == 1)
    def _():
        rest(0).wait_recv()
        rest(1).wait_recv()


def split(value):
    high = value.astype(jnp.bfloat16)
    low = (value - high.astype(jnp.float32)).astype(jnp.bfloat16)
    return high, low


def dot3(a, b):
    size = a.shape[0] // 2
    high, low = split(b)
    both = jnp.dot(a, high, preferred_element_type=jnp.float32)
    rest = jnp.dot(a[0:size], low, preferred_element_type=jnp.float32)
    return both[0:size] + (both[size:2 * size] + rest)


def apply_kernel(cols, inv, w, r, out, stage, factor, sems):
    parity = lax.axis_index("fac") % 2
    size = cols * 8
    width = w.shape[1]
    block = width // 4
    rows = jnp.where(parity == 0, inv[0:cols, :], inv[cols:2 * cols, :])
    rows = jnp.broadcast_to(rows[:, None, :], (cols, 8, LANES)).reshape(size, LANES)
    source = row_iota(LANES)
    target = lane_iota(LANES)
    same = (source % 8) == (target % 8)
    rows = jnp.concatenate(split(rows), 0)
    same = jnp.concatenate([same, same], 0)
    for part, first in ((0, parity * cols), (1, 0)):
        spread = (source == first + target // 8).astype(jnp.bfloat16)
        wide = jnp.dot(rows, spread, preferred_element_type=jnp.float32)
        factor[:, part * size:(part + 1) * size] = jnp.where(same, wide, 0.0).astype(jnp.bfloat16)

    def send(k):
        part = pl.ds(k * block, block)
        return pltpu.make_async_copy(stage.at[:, part], out.at[:, part], sems.at[k])

    @pl.when(parity == 0)
    def _():
        for k in range(4):
            part = pl.ds(k * block, block)
            stage[:, part] = dot3(factor[:, 0:size], w[:, part])
            send(k).start()

    @pl.when(parity == 1)
    def _():
        for k in range(4):
            part = pl.ds(k * block, block)
            both = jnp.concatenate([w[:, part], r[:, part]], 0)
            stage[:, part] = dot3(factor[...], both)
            send(k).start()

    for k in range(4):
        send(k).wait()


def per_device(tiles, panel, materials, table, shifts, shift_pick):
    cols, depth, width = panel.shape
    zs = tiles // LINE
    hbm = pl.BlockSpec(memory_space=pltpu.HBM)
    vmem = pl.BlockSpec(memory_space=pltpu.VMEM)
    dma = pltpu.SemaphoreType.DMA
    f32 = jnp.float32
    w, r, inv = pl.pallas_call(
        functools.partial(solve_kernel, tiles),
        name="solve",
        out_shape=(jax.ShapeDtypeStruct((cols, depth, width), f32), jax.ShapeDtypeStruct((cols, depth, width), f32),
                   jax.ShapeDtypeStruct((2 * cols, LANES), f32)),
        in_specs=[hbm] * 4 + [pl.BlockSpec(memory_space=pltpu.SMEM)],
        out_specs=(vmem, vmem, vmem),
        scratch_shapes=[
            pltpu.SMEM(table.shape, f32),
            pltpu.SMEM(shifts.shape, f32),
            pltpu.VMEM((cols, 16, width), f32),
            pltpu.VMEM((24, width), jnp.int32),
            pltpu.VMEM((6, 16, width), f32),
            pltpu.VMEM((16, width), f32),
            pltpu.VMEM((cols * depth, LANES), f32),
            pltpu.VMEM((GROUP, 8, LANES), f32),
            pltpu.VMEM((zs, 8, LANES), f32),
            pltpu.SemaphoreType.REGULAR((7,)),
            dma((2,)), dma, dma, dma((2,)), dma((2,)), dma((2, cols)), dma((2, cols)), dma((cols,)), dma((cols,)), dma((2,)), dma((2,)),
            dma((GROUP,)), dma((GROUP,)), dma((zs,)), dma((zs,)),
        ],
        compiler_params=pltpu.CompilerParams(collective_id=0, has_side_effects=True, vmem_limit_bytes=32 * 1024 * 1024),
    )(*(pltpu.with_memory_space_constraint(a, pltpu.HBM) for a in (panel, materials, table, shifts)), shift_pick)
    rows = cols * depth
    basis = pl.pallas_call(
        functools.partial(apply_kernel, cols),
        name="apply",
        out_shape=jax.ShapeDtypeStruct((rows, width), f32),
        in_specs=[vmem] * 3,
        out_specs=hbm,
        scratch_shapes=[pltpu.VMEM((rows, width), f32), pltpu.VMEM((2 * rows, 2 * rows), jnp.bfloat16), dma((4,))],
        compiler_params=pltpu.CompilerParams(vmem_limit_bytes=32 * 1024 * 1024),
    )(inv, w.reshape(rows, width), r.reshape(rows, width))
    return basis.reshape(cols, depth, width)


def solution(mesh):
    placed = (P("fac", "tile", None), P("tile", None), P(), P(), P())
    return jax.shard_map(
        functools.partial(per_device, mesh.shape["tile"]), mesh=mesh, in_specs=placed,
        out_specs=P("fac", "tile", None), check_vma=False,
    )
```

```python
import functools

import jax
import jax.numpy as jnp
from jax import lax
from jax.experimental import pallas as pl
from jax.experimental.pallas import tpu as pltpu
from jax.sharding import PartitionSpec as P

NZ = 64
SWEEPS = 4
OMEGA = 0.8
LANES = 128
YS = 4
CORES = 2
GROUP = 2 * YS * CORES
LINE = YS * CORES
HALO = 4
MESH = pl.DeviceIdType.MESH
HIGHEST = lax.Precision.HIGHEST


def chunked(value):
    return [value[:, i:i + LANES] for i in range(0, value.shape[1], LANES)]


def lane_iota(rows):
    return lax.broadcasted_iota(jnp.int32, (rows, LANES), 1)


def row_iota(rows):
    return lax.broadcasted_iota(jnp.int32, (rows, LANES), 0)


def pick_field(ids, table, field):
    low = (ids & 1) == 1
    mid = (ids & 2) == 2
    high = (ids & 4) == 4
    pairs = [jnp.where(low, table[field, i + 1], table[field, i]) for i in range(0, 8, 2)]
    quads = [jnp.where(mid, pairs[1], pairs[0]), jnp.where(mid, pairs[3], pairs[2])]
    return jnp.where(high, quads[1], quads[0])


def harmonic(first, second):
    return 2.0 * first * second / (first + second)


def plane_faces(ids, table, shift_value):
    count = len(ids)
    lane = lane_iota(8)
    left = lane < NZ
    top = (lane % NZ) == NZ - 1
    cond_y = [pick_field(i, table, 1) for i in ids]
    turned = [pltpu.roll(v, NZ, 1) for v in cond_y]
    faces_y = []
    for k in range(count):
        above = jnp.where(left, turned[k], turned[min(k + 1, count - 1)])
        face = harmonic(cond_y[k], above)
        faces_y.append(jnp.where(left, face, 0.0) if k == count - 1 else face)
    back_y = [pltpu.roll(v, NZ, 1) for v in faces_y]
    found = []
    for k in range(count):
        below = back_y[k - 1] if k else jnp.zeros_like(back_y[0])
        prev_y = jnp.where(left, below, back_y[k])
        cond_z = pick_field(ids[k], table, 2)
        next_z = jnp.where(top, 0.0, harmonic(cond_z, pltpu.roll(cond_z, LANES - 1, 1)))
        prev_z = pltpu.roll(next_z, 1, 1)
        capacity = pick_field(ids[k], table, 3)
        partial = shift_value * capacity + (prev_y + faces_y[k] + prev_z + next_z)
        found.append((prev_y, faces_y[k], prev_z, next_z, partial))
    return found


def own_coefficients(shift_value, ids_ref, table, coef, inv_ref, cond_ref):
    ids = chunked(ids_ref[0:8, :])
    for k, (prev_y, next_y, prev_z, next_z, partial) in enumerate(plane_faces(ids, table, shift_value)):
        where = pl.ds(k * LANES, LANES)
        cond = pick_field(ids[k], table, 0)
        coef[1, 0:8, where] = harmonic(cond, pltpu.roll(cond, 7, 0))
        for i, face in enumerate((prev_y, next_y, prev_z, next_z)):
            coef[2 + i, 0:8, where] = face
        inv_ref[0:8, where] = partial
        cond_ref[:, where] = cond


def all_coefficients(tiles, me, shift_value, ids_ref, table, coef, inv_ref, cond_ref):
    row = row_iota(8)
    after = chunked(ids_ref[8:16, :])
    before = chunked(ids_ref[16:24, :])
    halo = plane_faces([jnp.where(row < HALO, a, b) for a, b in zip(after, before)], table, shift_value)
    for k in range(len(after)):
        where = pl.ds(k * LANES, LANES)
        cond = cond_ref[:, where]
        cond_after = pick_field(after[k], table, 0)
        cond_before = pick_field(before[k], table, 0)
        middle = jnp.where(row < HALO, cond_after, cond_before)
        lower = jnp.where(row < HALO, pltpu.roll(cond_after, 1, 0), pltpu.roll(cond_before, 1, 0))
        lower = jnp.where(row == 0, pltpu.roll(cond, 1, 0), lower)
        upper = jnp.where(row < HALO, pltpu.roll(cond_after, 7, 0), pltpu.roll(cond_before, 7, 0))
        upper = jnp.where(row == 7, pltpu.roll(cond, 7, 0), upper)
        prev_halo = jnp.where((row == 0) & (me == tiles - 1), 0.0, harmonic(lower, middle))
        next_halo = jnp.where((row == 7) & (me == 0), 0.0, harmonic(middle, upper))
        inner = coef[1, 0:8, where]
        next_own = jnp.where(row == 7, pltpu.roll(prev_halo, 7, 0), inner)
        prev_own = jnp.where(row == 0, pltpu.roll(next_halo, 1, 0), pltpu.roll(inner, 1, 0))
        inverse = 1.0 / (inv_ref[0:8, where] + (prev_own + next_own))
        scaled = OMEGA * inverse
        coef[0, 0:8, where] = prev_own * scaled
        coef[1, 0:8, where] = next_own * scaled
        for i in range(2, 6):
            coef[i, 0:8, where] = coef[i, 0:8, where] * scaled
        inv_ref[0:8, where] = inverse
        inverse = 1.0 / (halo[k][4] + (prev_halo + next_halo))
        scaled = OMEGA * inverse
        for i, face in enumerate((prev_halo, next_halo) + halo[k][0:4]):
            coef[i, 8:16, where] = face * scaled
        inv_ref[8:16, where] = inverse


def solve_column(source_ref, coef, inv_ref):
    count = inv_ref.shape[1] // LANES
    where = [pl.ds(k * LANES, LANES) for k in range(count)]
    values = [source_ref[:, where[k]] * inv_ref[:, where[k]] for k in range(count)]
    base = [OMEGA * v for v in values]
    for sweep in range(SWEEPS):
        rows = 8 if sweep == SWEEPS - 1 else 16
        left = lane_iota(rows) < NZ
        centers = [v[0:rows] for v in values]
        turned = [pltpu.roll(v, NZ, 1) for v in centers]
        new = []
        for k in range(count):
            v = centers[k]
            total = (1.0 - OMEGA) * v + base[k][0:rows]
            total += coef[0, 0:rows, where[k]] * pltpu.roll(values[k], 1, 0)[0:rows]
            total += coef[1, 0:rows, where[k]] * pltpu.roll(values[k], 15, 0)[0:rows]
            below = jnp.where(left, turned[max(k - 1, 0)], turned[k])
            above = jnp.where(left, turned[k], turned[min(k + 1, count - 1)])
            total += coef[2, 0:rows, where[k]] * below
            total += coef[3, 0:rows, where[k]] * above
            total += coef[4, 0:rows, where[k]] * pltpu.roll(v, 1, 1)
            total += coef[5, 0:rows, where[k]] * pltpu.roll(v, LANES - 1, 1)
            new.append(total)
        values = new
    return values


def diagonal_blocks(product):
    size = product.shape[0]
    keep = (row_iota(size) % 8) == (lane_iota(size) % 8)
    kept = jnp.where(keep, product, 0.0)
    return jnp.sum(kept.reshape(size // 8, 8, LANES), axis=1)


def thirds(value):
    parts = []
    for _ in range(3):
        part = value.astype(jnp.bfloat16)
        parts.append(part)
        value = value - part.astype(jnp.float32)
    return jnp.concatenate(parts, 0)


def pack(value, first_row, first_column):
    source = lax.broadcasted_iota(jnp.int32, (LANES, LANES), 0)
    target = lax.broadcasted_iota(jnp.int32, (LANES, LANES), 1)
    places = []
    for half in range(2):
        place = (first_row + half * 8) * 4 + first_column + source // 8
        places.append((place == target).astype(jnp.bfloat16))
    left = jnp.concatenate([thirds(value[0:8]), thirds(value[8:16])], 1)
    found = jnp.dot(left, jnp.concatenate(places, 0), preferred_element_type=jnp.float32)
    return found[0:8] + (found[8:16] + found[16:24])


def inverse_factor(packed, size, out):
    count = size // 8
    row = row_iota(8)
    lane = lane_iota(8)

    def spread(value, r):
        return jnp.broadcast_to(value[r:r + 1, :], (8, LANES))

    left = {(j, q): jnp.broadcast_to(packed[:, 32 * q + j:32 * q + j + 1], (8, LANES))
            for j in range(size) for q in range(j // 8, count)}
    right = [jnp.where(lane == row + 8 * q, 1.0, 0.0) for q in range(count)]
    pivots = []
    for k in range(size):
        at, r = k // 8, k % 8
        pivot = 1.0 / spread(left[k, at], r)
        pivots.append(pivot)
        if k == size - 1:
            break
        scaled = {q: left[k, q] * pivot for q in range(at, count)}
        for j in range(k + 1, size):
            other = spread(scaled[j // 8], j % 8)
            for q in range(j // 8, count):
                left[j, q] = left[j, q] - left[k, q] * other
        source = spread(right[at], r)
        for q in range(at, count):
            factor = jnp.where(row > r, scaled[q], 0.0) if q == at else scaled[q]
            right[q] = right[q] - factor * source
    for q in range(count):
        scale = pivots[8 * q]
        for r in range(1, 8):
            scale = jnp.where(row == r, pivots[8 * q + r], scale)
        out[8 * q:8 * q + 8, :] = right[q] * jnp.sqrt(scale)


def solve_kernel(tiles, panel, ids, table_hbm, shifts_hbm, pick, w, r, inv_out, table, shifts,
                 ext, idx, coef, inv_ref, cond, cross, gbuf, zbuf, token,
                 scalar_sem, ids_sem, own_sem, ids_send, ids_recv, halo_send, halo_recv, swap_send, swap_recv, rest_send, rest_recv,
                 group_send, group_recv, line_send, line_recv):
    cols = panel.shape[0]
    width = panel.shape[2]
    half = width // 2
    zs = tiles // LINE
    me = lax.axis_index("tile")
    fac = lax.axis_index("fac")
    parity = fac % 2
    partner = fac + 1 - 2 * parity
    line = me // LINE
    spot = me % LINE
    before = lax.rem(me + tiles - 1, tiles)
    after = lax.rem(me + 1, tiles)
    seat = parity * LINE + spot

    scalars = [pltpu.make_async_copy(a, b, scalar_sem.at[i])
               for i, (a, b) in enumerate(((table_hbm, table), (shifts_hbm, shifts)))]
    own_ids = pltpu.make_async_copy(ids, idx.at[pl.ds(0, 8)], ids_sem)

    def group_peer(step):
        core = lax.rem(spot % CORES + step % CORES, CORES)
        y = lax.rem(spot // CORES + step // CORES % YS, YS)
        x = lax.rem(parity + step // LINE, 2)
        return {"tile": line * LINE + y * CORES + core, "fac": fac - parity + x}, x * LINE + y * CORES + core

    def group_distance(step):
        y = step // CORES % YS
        return step // LINE + min(y, YS - y) + 0.5 * (step % CORES)

    def line_peer(step):
        there = lax.rem(line + step, zs)
        return {"tile": there * LINE + spot, "fac": fac}, there

    def along(distance):
        return {"tile": lax.rem(line + distance + zs, zs) * LINE + spot, "fac": fac}

    barrier = pltpu.get_barrier_semaphore()
    near = {"tile": me, "fac": partner}
    greeted = [{"tile": before, "fac": fac}, {"tile": after, "fac": fac}, near]
    greeted += [{"tile": line * LINE + lax.rem(spot + i, LINE), "fac": fac} for i in range(1, LINE)]
    greeted += [along(i) for i in (-2, -1, 1, 2)]
    for peer in greeted:
        pl.semaphore_signal(barrier, inc=1, device_id=peer, device_id_type=MESH)
    for copy in scalars + [own_ids]:
        copy.start()
    pl.semaphore_wait(barrier, len(greeted))

    def greet(turn):
        pl.semaphore_signal(token.at[2 * turn], inc=1, device_id=along(2), device_id_type=MESH)
        pl.semaphore_signal(token.at[2 * turn + 1], inc=1, device_id=along(-2), device_id_type=MESH)

    def greeted_by(turn):
        pl.semaphore_wait(token.at[2 * turn], 1)
        pl.semaphore_wait(token.at[2 * turn + 1], 1)

    ids_up = pltpu.make_async_remote_copy(ids.at[pl.ds(3, 5)], idx.at[pl.ds(19, 5)], ids_send.at[0], ids_recv.at[0],
                                          device_id={"tile": after, "fac": fac}, device_id_type=MESH)
    ids_down = pltpu.make_async_remote_copy(ids.at[pl.ds(0, 5)], idx.at[pl.ds(8, 5)], ids_send.at[1], ids_recv.at[1],
                                            device_id={"tile": before, "fac": fac}, device_id_type=MESH)
    ids_up.start()
    ids_down.start()

    def halo_up(c):
        return pltpu.make_async_remote_copy(panel.at[c, pl.ds(8 - HALO, HALO)], ext.at[c, pl.ds(8 + HALO, HALO)],
                                            halo_send.at[0, c], halo_recv.at[0, c],
                                            device_id={"tile": after, "fac": fac}, device_id_type=MESH)

    def halo_down(c):
        return pltpu.make_async_remote_copy(panel.at[c, pl.ds(0, HALO)], ext.at[c, pl.ds(8, HALO)],
                                            halo_send.at[1, c], halo_recv.at[1, c],
                                            device_id={"tile": before, "fac": fac}, device_id_type=MESH)

    def own_column(c):
        return pltpu.make_async_copy(panel.at[c], ext.at[c, pl.ds(0, 8)], own_sem.at[c])

    def send_halo(c, carry):
        halo_up(c).start()
        halo_down(c).start()
        own_column(c).start()
        return carry

    lax.fori_loop(0, cols, send_halo, 0)

    giving = pl.ds(pl.multiple_of(parity * half, half), half)

    def swap(c):
        return pltpu.make_async_remote_copy(w.at[c, :, giving], r.at[c, :, giving], swap_send.at[c], swap_recv.at[c],
                                            device_id={"tile": me, "fac": partner}, device_id_type=MESH)

    pl.semaphore_signal(token.at[6], inc=1, device_id=near, device_id_type=MESH)
    greet(0)
    for copy in scalars:
        copy.wait()
    shift_value = shifts[pick[0]]
    own_ids.wait()
    own_coefficients(shift_value, idx, table, coef, inv_ref, cond)
    ids_up.wait()
    ids_down.wait()
    all_coefficients(tiles, me, shift_value, idx, table, coef, inv_ref, cond)

    def column(c, carry):
        halo_up(c).wait()
        halo_down(c).wait()
        own_column(c).wait()

        @pl.when(c > 0)
        def _():
            swap(c - 1).start()

        for turn in range(3):
            @pl.when(c == 4 * (turn + 1))
            def _():
                greeted_by(turn)
                if turn < 2:
                    greet(turn + 1)

        values = solve_column(ext.at[c], coef, inv_ref)
        for k, value in enumerate(values):
            w[c, :, pl.ds(k * LANES, LANES)] = value
        return carry

    lax.fori_loop(0, cols, column, 0)
    def rest(part):
        some = pl.ds(0, cols // 4) if part == 0 else pl.ds(cols // 4, cols - cols // 4)
        side = pl.ds(half, half)
        return pltpu.make_async_remote_copy(w.at[some, :, side], r.at[some, :, side], rest_send.at[part], rest_recv.at[part],
                                            device_id=near, device_id_type=MESH)

    own = w[...].reshape(cols * 8, width)
    gram = lax.dot_general(own, own, (((1,), (1,)), ((), ())), precision=HIGHEST, preferred_element_type=jnp.float32)
    swap(cols - 1).start()

    @pl.when(parity == 0)
    def _():
        rest(0).start()

    own_packed = pack(diagonal_blocks(gram), parity * cols, parity * cols)

    def arrived(c, carry):
        swap(c).wait()
        return carry

    def product(a, b):
        return lax.dot_general(a, b, (((1,), (1,)), ((), ())), precision=HIGHEST, preferred_element_type=jnp.float32)

    early = cols - cols // 4
    for first, last in ((0, early), (early, cols)):
        lax.fori_loop(first, last, arrived, 0)

        @pl.when(parity == 0)
        def _():
            mine = w[:, :, half:].reshape(cols * 8, half)
            cross[8 * first:8 * last, :] = product(r[first:last, :, half:].reshape((last - first) * 8, half), mine)

        @pl.when(parity == 1)
        def _():
            mine = w[:, :, 0:half].reshape(cols * 8, half)
            cross[:, 8 * first:8 * last] = product(mine, r[first:last, :, 0:half].reshape((last - first) * 8, half))

    gbuf[seat] = own_packed + pack(diagonal_blocks(cross[...]), cols, 0)

    def group_copy(step):
        peer, _ = group_peer(step)
        return pltpu.make_async_remote_copy(gbuf.at[seat], gbuf.at[seat], group_send.at[step], group_recv.at[seat],
                                            device_id=peer, device_id_type=MESH)

    def group_arrival(step):
        peer, there = group_peer(step)
        return pltpu.make_async_remote_copy(gbuf.at[there], gbuf.at[there], group_send.at[step], group_recv.at[there],
                                            device_id=peer, device_id_type=MESH)

    def line_copy(step):
        peer, _ = line_peer(step)
        return pltpu.make_async_remote_copy(zbuf.at[line], zbuf.at[line], line_send.at[step], line_recv.at[line],
                                            device_id=peer, device_id_type=MESH)

    def line_arrival(step):
        peer, there = line_peer(step)
        return pltpu.make_async_remote_copy(zbuf.at[there], zbuf.at[there], line_send.at[step], line_recv.at[there],
                                            device_id=peer, device_id_type=MESH)

    pl.semaphore_wait(token.at[6], 1)
    for step in sorted(range(1, GROUP), key=group_distance, reverse=True):
        group_copy(step).start()

    @pl.when(parity == 0)
    def _():
        rest(1).start()

    for step in range(1, GROUP):
        group_arrival(step).wait_recv()
    total = gbuf[0]
    for i in range(1, GROUP):
        total = total + gbuf[i]
    zbuf[line] = total
    order = sorted(range(1, zs), key=lambda s: -min(s, zs - s))
    for step in order:
        line_copy(step).start()
    for step in range(1, zs):
        line_arrival(step).wait_recv()
    total = zbuf[0]
    for i in range(1, zs):
        total = total + zbuf[i]
    cells = 8 * tiles * width
    inverse_factor(total / cells, 2 * cols, inv_out)

    for step in range(1, GROUP):
        group_copy(step).wait_send()
    for step in range(1, zs):
        line_copy(step).wait_send()

    @pl.when(parity == 0)
    def _():
        rest(0).wait_send()
        rest(1).wait_send()

    @pl.when(parity == 1)
    def _():
        rest(0).wait_recv()
        rest(1).wait_recv()


def split(value):
    high = value.astype(jnp.bfloat16)
    low = (value - high.astype(jnp.float32)).astype(jnp.bfloat16)
    return high, low


def dot3(a, b):
    size = a.shape[0] // 2
    high, low = split(b)
    both = jnp.dot(a, high, preferred_element_type=jnp.float32)
    rest = jnp.dot(a[0:size], low, preferred_element_type=jnp.float32)
    return both[0:size] + (both[size:2 * size] + rest)


def apply_kernel(cols, inv, w, r, out, stage, factor, sems):
    parity = lax.axis_index("fac") % 2
    size = cols * 8
    width = w.shape[1]
    block = width // 4
    rows = jnp.where(parity == 0, inv[0:cols, :], inv[cols:2 * cols, :])
    rows = jnp.broadcast_to(rows[:, None, :], (cols, 8, LANES)).reshape(size, LANES)
    source = row_iota(LANES)
    target = lane_iota(LANES)
    same = (source % 8) == (target % 8)
    rows = jnp.concatenate(split(rows), 0)
    same = jnp.concatenate([same, same], 0)
    for part, first in ((0, parity * cols), (1, 0)):
        spread = (source == first + target // 8).astype(jnp.bfloat16)
        wide = jnp.dot(rows, spread, preferred_element_type=jnp.float32)
        factor[:, part * size:(part + 1) * size] = jnp.where(same, wide, 0.0).astype(jnp.bfloat16)

    def send(k):
        part = pl.ds(k * block, block)
        return pltpu.make_async_copy(stage.at[:, part], out.at[:, part], sems.at[k])

    @pl.when(parity == 0)
    def _():
        for k in range(4):
            part = pl.ds(k * block, block)
            stage[:, part] = dot3(factor[:, 0:size], w[:, part])
            send(k).start()

    @pl.when(parity == 1)
    def _():
        for k in range(4):
            part = pl.ds(k * block, block)
            both = jnp.concatenate([w[:, part], r[:, part]], 0)
            stage[:, part] = dot3(factor[...], both)
            send(k).start()

    for k in range(4):
        send(k).wait()


def per_device(tiles, panel, materials, table, shifts, shift_pick):
    cols, depth, width = panel.shape
    zs = tiles // LINE
    hbm = pl.BlockSpec(memory_space=pltpu.HBM)
    vmem = pl.BlockSpec(memory_space=pltpu.VMEM)
    dma = pltpu.SemaphoreType.DMA
    f32 = jnp.float32
    w, r, inv = pl.pallas_call(
        functools.partial(solve_kernel, tiles),
        name="solve",
        out_shape=(jax.ShapeDtypeStruct((cols, depth, width), f32), jax.ShapeDtypeStruct((cols, depth, width), f32),
                   jax.ShapeDtypeStruct((2 * cols, LANES), f32)),
        in_specs=[hbm] * 4 + [pl.BlockSpec(memory_space=pltpu.SMEM)],
        out_specs=(vmem, vmem, vmem),
        scratch_shapes=[
            pltpu.SMEM(table.shape, f32),
            pltpu.SMEM(shifts.shape, f32),
            pltpu.VMEM((cols, 16, width), f32),
            pltpu.VMEM((24, width), jnp.int32),
            pltpu.VMEM((6, 16, width), f32),
            pltpu.VMEM((16, width), f32),
            pltpu.VMEM((8, width), f32),
            pltpu.VMEM((cols * depth, LANES), f32),
            pltpu.VMEM((GROUP, 8, LANES), f32),
            pltpu.VMEM((zs, 8, LANES), f32),
            pltpu.SemaphoreType.REGULAR((7,)),
            dma((2,)), dma, dma((cols,)), dma((2,)), dma((2,)), dma((2, cols)), dma((2, cols)), dma((cols,)), dma((cols,)), dma((2,)), dma((2,)),
            dma((GROUP,)), dma((GROUP,)), dma((zs,)), dma((zs,)),
        ],
        compiler_params=pltpu.CompilerParams(collective_id=0, has_side_effects=True, vmem_limit_bytes=32 * 1024 * 1024),
    )(*(pltpu.with_memory_space_constraint(a, pltpu.HBM) for a in (panel, materials, table, shifts)), shift_pick)
    rows = cols * depth
    basis = pl.pallas_call(
        functools.partial(apply_kernel, cols),
        name="apply",
        out_shape=jax.ShapeDtypeStruct((rows, width), f32),
        in_specs=[vmem] * 3,
        out_specs=hbm,
        scratch_shapes=[pltpu.VMEM((rows, width), f32), pltpu.VMEM((2 * rows, 2 * rows), jnp.bfloat16), dma((4,))],
        compiler_params=pltpu.CompilerParams(vmem_limit_bytes=32 * 1024 * 1024),
    )(inv, w.reshape(rows, width), r.reshape(rows, width))
    return basis.reshape(cols, depth, width)


def solution(mesh):
    placed = (P("fac", "tile", None), P("tile", None), P(), P(), P())
    return jax.shard_map(
        functools.partial(per_device, mesh.shape["tile"]), mesh=mesh, in_specs=placed,
        out_specs=P("fac", "tile", None), check_vma=False,
    )
```

```python
import functools

import jax
import jax.numpy as jnp
from jax import lax
from jax.experimental import pallas as pl
from jax.experimental.pallas import tpu as pltpu
from jax.sharding import PartitionSpec as P

NZ = 64
SWEEPS = 4
OMEGA = 0.8
LANES = 128
YS = 4
CORES = 2
GROUP = 2 * YS * CORES
LINE = YS * CORES
HALO = 4
MESH = pl.DeviceIdType.MESH
HIGHEST = lax.Precision.HIGHEST


def chunked(value):
    return [value[:, i:i + LANES] for i in range(0, value.shape[1], LANES)]


def lane_iota(rows):
    return lax.broadcasted_iota(jnp.int32, (rows, LANES), 1)


def row_iota(rows):
    return lax.broadcasted_iota(jnp.int32, (rows, LANES), 0)


def pick_field(ids, table, field):
    low = (ids & 1) == 1
    mid = (ids & 2) == 2
    high = (ids & 4) == 4
    pairs = [jnp.where(low, table[field, i + 1], table[field, i]) for i in range(0, 8, 2)]
    quads = [jnp.where(mid, pairs[1], pairs[0]), jnp.where(mid, pairs[3], pairs[2])]
    return jnp.where(high, quads[1], quads[0])


def harmonic(first, second):
    return 2.0 * first * second / (first + second)


def plane_faces(ids, table, shift_value):
    count = len(ids)
    lane = lane_iota(8)
    left = lane < NZ
    top = (lane % NZ) == NZ - 1
    cond_y = [pick_field(i, table, 1) for i in ids]
    turned = [pltpu.roll(v, NZ, 1) for v in cond_y]
    faces_y = []
    for k in range(count):
        above = jnp.where(left, turned[k], turned[min(k + 1, count - 1)])
        face = harmonic(cond_y[k], above)
        faces_y.append(jnp.where(left, face, 0.0) if k == count - 1 else face)
    back_y = [pltpu.roll(v, NZ, 1) for v in faces_y]
    found = []
    for k in range(count):
        below = back_y[k - 1] if k else jnp.zeros_like(back_y[0])
        prev_y = jnp.where(left, below, back_y[k])
        cond_z = pick_field(ids[k], table, 2)
        next_z = jnp.where(top, 0.0, harmonic(cond_z, pltpu.roll(cond_z, LANES - 1, 1)))
        prev_z = pltpu.roll(next_z, 1, 1)
        capacity = pick_field(ids[k], table, 3)
        partial = shift_value * capacity + (prev_y + faces_y[k] + prev_z + next_z)
        found.append((prev_y, faces_y[k], prev_z, next_z, partial))
    return found


def own_coefficients(shift_value, ids_ref, table, coef, inv_ref, cond_ref):
    ids = chunked(ids_ref[0:8, :])
    for k, (prev_y, next_y, prev_z, next_z, partial) in enumerate(plane_faces(ids, table, shift_value)):
        where = pl.ds(k * LANES, LANES)
        cond = pick_field(ids[k], table, 0)
        coef[1, 0:8, where] = harmonic(cond, pltpu.roll(cond, 7, 0))
        for i, face in enumerate((prev_y, next_y, prev_z, next_z)):
            coef[2 + i, 0:8, where] = face
        inv_ref[0:8, where] = partial
        cond_ref[:, where] = cond


def all_coefficients(tiles, me, shift_value, ids_ref, table, coef, inv_ref, cond_ref):
    row = row_iota(8)
    after = chunked(ids_ref[8:16, :])
    before = chunked(ids_ref[16:24, :])
    halo = plane_faces([jnp.where(row < HALO, a, b) for a, b in zip(after, before)], table, shift_value)
    for k in range(len(after)):
        where = pl.ds(k * LANES, LANES)
        cond = cond_ref[:, where]
        cond_after = pick_field(after[k], table, 0)
        cond_before = pick_field(before[k], table, 0)
        middle = jnp.where(row < HALO, cond_after, cond_before)
        lower = jnp.where(row < HALO, pltpu.roll(cond_after, 1, 0), pltpu.roll(cond_before, 1, 0))
        lower = jnp.where(row == 0, pltpu.roll(cond, 1, 0), lower)
        upper = jnp.where(row < HALO, pltpu.roll(cond_after, 7, 0), pltpu.roll(cond_before, 7, 0))
        upper = jnp.where(row == 7, pltpu.roll(cond, 7, 0), upper)
        prev_halo = jnp.where((row == 0) & (me == tiles - 1), 0.0, harmonic(lower, middle))
        next_halo = jnp.where((row == 7) & (me == 0), 0.0, harmonic(middle, upper))
        inner = coef[1, 0:8, where]
        next_own = jnp.where(row == 7, pltpu.roll(prev_halo, 7, 0), inner)
        prev_own = jnp.where(row == 0, pltpu.roll(next_halo, 1, 0), pltpu.roll(inner, 1, 0))
        inverse = 1.0 / (inv_ref[0:8, where] + (prev_own + next_own))
        scaled = OMEGA * inverse
        coef[0, 0:8, where] = prev_own * scaled
        coef[1, 0:8, where] = next_own * scaled
        for i in range(2, 6):
            coef[i, 0:8, where] = coef[i, 0:8, where] * scaled
        inv_ref[0:8, where] = inverse
        inverse = 1.0 / (halo[k][4] + (prev_halo + next_halo))
        scaled = OMEGA * inverse
        for i, face in enumerate((prev_halo, next_halo) + halo[k][0:4]):
            coef[i, 8:16, where] = face * scaled
        inv_ref[8:16, where] = inverse


def solve_column(source_ref, coef, inv_ref):
    count = inv_ref.shape[1] // LANES
    where = [pl.ds(k * LANES, LANES) for k in range(count)]
    values = [source_ref[:, where[k]] * inv_ref[:, where[k]] for k in range(count)]
    base = [OMEGA * v for v in values]
    for sweep in range(SWEEPS):
        rows = 8 if sweep == SWEEPS - 1 else 16
        left = lane_iota(rows) < NZ
        centers = [v[0:rows] for v in values]
        turned = [pltpu.roll(v, NZ, 1) for v in centers]
        new = []
        for k in range(count):
            v = centers[k]
            total = (1.0 - OMEGA) * v + base[k][0:rows]
            total += coef[0, 0:rows, where[k]] * pltpu.roll(values[k], 1, 0)[0:rows]
            total += coef[1, 0:rows, where[k]] * pltpu.roll(values[k], 15, 0)[0:rows]
            below = jnp.where(left, turned[max(k - 1, 0)], turned[k])
            above = jnp.where(left, turned[k], turned[min(k + 1, count - 1)])
            total += coef[2, 0:rows, where[k]] * below
            total += coef[3, 0:rows, where[k]] * above
            total += coef[4, 0:rows, where[k]] * pltpu.roll(v, 1, 1)
            total += coef[5, 0:rows, where[k]] * pltpu.roll(v, LANES - 1, 1)
            new.append(total)
        values = new
    return values


def diagonal_blocks(product):
    size = product.shape[0]
    keep = (row_iota(size) % 8) == (lane_iota(size) % 8)
    kept = jnp.where(keep, product, 0.0)
    return jnp.sum(kept.reshape(size // 8, 8, LANES), axis=1)


def thirds(value):
    parts = []
    for _ in range(3):
        part = value.astype(jnp.bfloat16)
        parts.append(part)
        value = value - part.astype(jnp.float32)
    return jnp.concatenate(parts, 0)


def pack(value, first_row, first_column):
    source = lax.broadcasted_iota(jnp.int32, (LANES, LANES), 0)
    target = lax.broadcasted_iota(jnp.int32, (LANES, LANES), 1)
    places = []
    for half in range(2):
        place = (first_row + half * 8) * 4 + first_column + source // 8
        places.append((place == target).astype(jnp.bfloat16))
    left = jnp.concatenate([thirds(value[0:8]), thirds(value[8:16])], 1)
    found = jnp.dot(left, jnp.concatenate(places, 0), preferred_element_type=jnp.float32)
    return found[0:8] + (found[8:16] + found[16:24])


def inverse_factor(packed, size, out):
    count = size // 8
    row = row_iota(8)
    lane = lane_iota(8)

    def spread(value, r):
        return jnp.broadcast_to(value[r:r + 1, :], (8, LANES))

    left = {(j, q): jnp.broadcast_to(packed[:, 32 * q + j:32 * q + j + 1], (8, LANES))
            for j in range(size) for q in range(j // 8, count)}
    right = [jnp.where(lane == row + 8 * q, 1.0, 0.0) for q in range(count)]
    pivots = []
    for k in range(size):
        at, r = k // 8, k % 8
        pivot = 1.0 / spread(left[k, at], r)
        pivots.append(pivot)
        if k == size - 1:
            break
        scaled = {q: left[k, q] * pivot for q in range(at, count)}
        for j in range(k + 1, size):
            other = spread(scaled[j // 8], j % 8)
            for q in range(j // 8, count):
                left[j, q] = left[j, q] - left[k, q] * other
        source = spread(right[at], r)
        for q in range(at, count):
            factor = jnp.where(row > r, scaled[q], 0.0) if q == at else scaled[q]
            right[q] = right[q] - factor * source
    for q in range(count):
        scale = pivots[8 * q]
        for r in range(1, 8):
            scale = jnp.where(row == r, pivots[8 * q + r], scale)
        out[8 * q:8 * q + 8, :] = right[q] * jnp.sqrt(scale)


def solve_kernel(tiles, panel, ids, table_hbm, shifts_hbm, pick, w, r, inv_out, table, shifts,
                 ext, idx, coef, inv_ref, cond, cross, gbuf, zbuf, token,
                 scalar_sem, ids_sem, own_sem, ids_send, ids_recv, halo_send, halo_recv, swap_send, swap_recv, rest_send, rest_recv,
                 group_send, group_recv, line_send, line_recv):
    cols = panel.shape[0]
    width = panel.shape[2]
    half = width // 2
    zs = tiles // LINE
    me = lax.axis_index("tile")
    fac = lax.axis_index("fac")
    parity = fac % 2
    partner = fac + 1 - 2 * parity
    line = me // LINE
    spot = me % LINE
    before = lax.rem(me + tiles - 1, tiles)
    after = lax.rem(me + 1, tiles)
    seat = parity * LINE + spot

    scalars = [pltpu.make_async_copy(a, b, scalar_sem.at[i])
               for i, (a, b) in enumerate(((table_hbm, table), (shifts_hbm, shifts)))]
    own_ids = pltpu.make_async_copy(ids, idx.at[pl.ds(0, 8)], ids_sem)

    def group_peer(step):
        core = lax.rem(spot % CORES + step % CORES, CORES)
        y = lax.rem(spot // CORES + step // CORES % YS, YS)
        x = lax.rem(parity + step // LINE, 2)
        return {"tile": line * LINE + y * CORES + core, "fac": fac - parity + x}, x * LINE + y * CORES + core

    def group_distance(step):
        y = step // CORES % YS
        return step // LINE + min(y, YS - y) + 0.5 * (step % CORES)

    def line_peer(step):
        there = lax.rem(line + step, zs)
        return {"tile": there * LINE + spot, "fac": fac}, there

    def along(distance):
        return {"tile": lax.rem(line + distance + zs, zs) * LINE + spot, "fac": fac}

    barrier = pltpu.get_barrier_semaphore()
    near = {"tile": me, "fac": partner}
    greeted = [{"tile": before, "fac": fac}, {"tile": after, "fac": fac}, near]
    greeted += [{"tile": line * LINE + lax.rem(spot + i, LINE), "fac": fac} for i in range(1, LINE)]
    greeted += [along(i) for i in (-2, -1, 1, 2)]
    for peer in greeted:
        pl.semaphore_signal(barrier, inc=1, device_id=peer, device_id_type=MESH)
    for copy in scalars + [own_ids]:
        copy.start()
    pl.semaphore_wait(barrier, len(greeted))

    def greet(turn):
        pl.semaphore_signal(token.at[2 * turn], inc=1, device_id=along(2), device_id_type=MESH)
        pl.semaphore_signal(token.at[2 * turn + 1], inc=1, device_id=along(-2), device_id_type=MESH)

    def greeted_by(turn):
        pl.semaphore_wait(token.at[2 * turn], 1)
        pl.semaphore_wait(token.at[2 * turn + 1], 1)

    ids_up = pltpu.make_async_remote_copy(ids.at[pl.ds(3, 5)], idx.at[pl.ds(19, 5)], ids_send.at[0], ids_recv.at[0],
                                          device_id={"tile": after, "fac": fac}, device_id_type=MESH)
    ids_down = pltpu.make_async_remote_copy(ids.at[pl.ds(0, 5)], idx.at[pl.ds(8, 5)], ids_send.at[1], ids_recv.at[1],
                                            device_id={"tile": before, "fac": fac}, device_id_type=MESH)
    ids_up.start()
    ids_down.start()

    def halo_up(c):
        return pltpu.make_async_remote_copy(panel.at[c, pl.ds(8 - HALO, HALO)], ext.at[c, pl.ds(8 + HALO, HALO)],
                                            halo_send.at[0, c], halo_recv.at[0, c],
                                            device_id={"tile": after, "fac": fac}, device_id_type=MESH)

    def halo_down(c):
        return pltpu.make_async_remote_copy(panel.at[c, pl.ds(0, HALO)], ext.at[c, pl.ds(8, HALO)],
                                            halo_send.at[1, c], halo_recv.at[1, c],
                                            device_id={"tile": before, "fac": fac}, device_id_type=MESH)

    def own_column(c):
        return pltpu.make_async_copy(panel.at[c], ext.at[c, pl.ds(0, 8)], own_sem.at[c])

    def send_halo(c, carry):
        halo_up(c).start()
        halo_down(c).start()
        own_column(c).start()
        return carry

    lax.fori_loop(0, cols, send_halo, 0)

    giving = pl.ds(pl.multiple_of(parity * half, half), half)

    def swap(c):
        return pltpu.make_async_remote_copy(w.at[c, :, giving], r.at[c, :, giving], swap_send.at[c], swap_recv.at[c],
                                            device_id={"tile": me, "fac": partner}, device_id_type=MESH)

    pl.semaphore_signal(token.at[6], inc=1, device_id=near, device_id_type=MESH)
    greet(0)
    for copy in scalars:
        copy.wait()
    shift_value = shifts[pick[0]]
    own_ids.wait()
    own_coefficients(shift_value, idx, table, coef, inv_ref, cond)
    ids_up.wait()
    ids_down.wait()
    all_coefficients(tiles, me, shift_value, idx, table, coef, inv_ref, cond)

    def column(c, carry):
        halo_up(c).wait()
        halo_down(c).wait()
        own_column(c).wait()

        @pl.when(c > 0)
        def _():
            swap(c - 1).start()

        for turn in range(3):
            @pl.when(c == 4 * (turn + 1))
            def _():
                greeted_by(turn)
                if turn < 2:
                    greet(turn + 1)

        values = solve_column(ext.at[c], coef, inv_ref)
        for k, value in enumerate(values):
            w[c, :, pl.ds(k * LANES, LANES)] = value
        return carry

    lax.fori_loop(0, cols, column, 0)
    def rest(part):
        some = pl.ds(0, cols // 4) if part == 0 else pl.ds(cols // 4, cols - cols // 4)
        side = pl.ds(half, half)
        return pltpu.make_async_remote_copy(w.at[some, :, side], r.at[some, :, side], rest_send.at[part], rest_recv.at[part],
                                            device_id=near, device_id_type=MESH)

    own = w[...].reshape(cols * 8, width)
    gram = lax.dot_general(own, own, (((1,), (1,)), ((), ())), precision=HIGHEST, preferred_element_type=jnp.float32)
    swap(cols - 1).start()

    @pl.when(parity == 0)
    def _():
        rest(0).start()

    own_packed = pack(diagonal_blocks(gram), parity * cols, parity * cols)

    def arrived(c, carry):
        swap(c).wait()
        return carry

    def product(a, b):
        return lax.dot_general(a, b, (((1,), (1,)), ((), ())), precision=HIGHEST, preferred_element_type=jnp.float32)

    early = cols - cols // 4
    for first, last in ((0, early), (early, cols)):
        lax.fori_loop(first, last, arrived, 0)

        @pl.when(parity == 0)
        def _():
            mine = w[:, :, half:].reshape(cols * 8, half)
            cross[8 * first:8 * last, :] = product(r[first:last, :, half:].reshape((last - first) * 8, half), mine)

        @pl.when(parity == 1)
        def _():
            mine = w[:, :, 0:half].reshape(cols * 8, half)
            cross[:, 8 * first:8 * last] = product(mine, r[first:last, :, 0:half].reshape((last - first) * 8, half))

    gbuf[seat] = own_packed + pack(diagonal_blocks(cross[...]), cols, 0)

    def group_copy(step):
        peer, _ = group_peer(step)
        return pltpu.make_async_remote_copy(gbuf.at[seat], gbuf.at[seat], group_send.at[step], group_recv.at[seat],
                                            device_id=peer, device_id_type=MESH)

    def group_arrival(step):
        peer, there = group_peer(step)
        return pltpu.make_async_remote_copy(gbuf.at[there], gbuf.at[there], group_send.at[step], group_recv.at[there],
                                            device_id=peer, device_id_type=MESH)

    def line_copy(step):
        peer, _ = line_peer(step)
        return pltpu.make_async_remote_copy(zbuf.at[line], zbuf.at[line], line_send.at[step], line_recv.at[line],
                                            device_id=peer, device_id_type=MESH)

    def line_arrival(step):
        peer, there = line_peer(step)
        return pltpu.make_async_remote_copy(zbuf.at[there], zbuf.at[there], line_send.at[step], line_recv.at[there],
                                            device_id=peer, device_id_type=MESH)

    pl.semaphore_wait(token.at[6], 1)

    def outward(steps):
        return sorted(steps, key=group_distance, reverse=True)

    @pl.when(parity == 0)
    def _():
        for step in outward(range(1, GROUP)):
            group_copy(step).start()
        rest(1).start()

    @pl.when(parity == 1)
    def _():
        for step in outward(range(1, LINE)):
            group_copy(step).start()

    for step in range(1, LINE):
        group_arrival(step).wait_recv()

    def group_sum(count):
        total = gbuf[0]
        for i in range(1, count):
            total = total + gbuf[i]
        zbuf[line] = total

    @pl.when(parity == 0)
    def _():
        group_sum(LINE)

    @pl.when(parity == 1)
    def _():
        for step in range(LINE, GROUP):
            group_arrival(step).wait_recv()
        group_sum(GROUP)

    order = sorted(range(1, zs), key=lambda s: -min(s, zs - s))
    for step in order:
        line_copy(step).start()
    for step in range(1, zs):
        line_arrival(step).wait_recv()
    total = zbuf[0]
    for i in range(1, zs):
        total = total + zbuf[i]
    cells = 8 * tiles * width

    @pl.when(parity == 0)
    def _():
        inverse_factor(total / cells, cols, inv_out)

    @pl.when(parity == 1)
    def _():
        inverse_factor(total / cells, 2 * cols, inv_out)

    for step in range(1, LINE):
        group_copy(step).wait_send()
    for step in range(1, zs):
        line_copy(step).wait_send()

    @pl.when(parity == 0)
    def _():
        for step in range(LINE, GROUP):
            group_copy(step).wait_send()
        rest(0).wait_send()
        rest(1).wait_send()

    @pl.when(parity == 1)
    def _():
        rest(0).wait_recv()
        rest(1).wait_recv()


def split(value):
    high = value.astype(jnp.bfloat16)
    low = (value - high.astype(jnp.float32)).astype(jnp.bfloat16)
    return high, low


def dot3(a, b):
    size = a.shape[0] // 2
    high, low = split(b)
    both = jnp.dot(a, high, preferred_element_type=jnp.float32)
    rest = jnp.dot(a[0:size], low, preferred_element_type=jnp.float32)
    return both[0:size] + (both[size:2 * size] + rest)


def apply_kernel(cols, inv, w, r, out, stage, factor, sems):
    parity = lax.axis_index("fac") % 2
    size = cols * 8
    width = w.shape[1]
    block = width // 4
    rows = jnp.where(parity == 0, inv[0:cols, :], inv[cols:2 * cols, :])
    rows = jnp.broadcast_to(rows[:, None, :], (cols, 8, LANES)).reshape(size, LANES)
    source = row_iota(LANES)
    target = lane_iota(LANES)
    same = (source % 8) == (target % 8)
    rows = jnp.concatenate(split(rows), 0)
    same = jnp.concatenate([same, same], 0)
    for part, first in ((0, parity * cols), (1, 0)):
        spread = (source == first + target // 8).astype(jnp.bfloat16)
        wide = jnp.dot(rows, spread, preferred_element_type=jnp.float32)
        factor[:, part * size:(part + 1) * size] = jnp.where(same, wide, 0.0).astype(jnp.bfloat16)

    def send(k):
        part = pl.ds(k * block, block)
        return pltpu.make_async_copy(stage.at[:, part], out.at[:, part], sems.at[k])

    @pl.when(parity == 0)
    def _():
        for k in range(4):
            part = pl.ds(k * block, block)
            stage[:, part] = dot3(factor[:, 0:size], w[:, part])
            send(k).start()

    @pl.when(parity == 1)
    def _():
        for k in range(4):
            part = pl.ds(k * block, block)
            both = jnp.concatenate([w[:, part], r[:, part]], 0)
            stage[:, part] = dot3(factor[...], both)
            send(k).start()

    for k in range(4):
        send(k).wait()


def per_device(tiles, panel, materials, table, shifts, shift_pick):
    cols, depth, width = panel.shape
    zs = tiles // LINE
    hbm = pl.BlockSpec(memory_space=pltpu.HBM)
    vmem = pl.BlockSpec(memory_space=pltpu.VMEM)
    dma = pltpu.SemaphoreType.DMA
    f32 = jnp.float32
    w, r, inv = pl.pallas_call(
        functools.partial(solve_kernel, tiles),
        name="solve",
        out_shape=(jax.ShapeDtypeStruct((cols, depth, width), f32), jax.ShapeDtypeStruct((cols, depth, width), f32),
                   jax.ShapeDtypeStruct((2 * cols, LANES), f32)),
        in_specs=[hbm] * 4 + [pl.BlockSpec(memory_space=pltpu.SMEM)],
        out_specs=(vmem, vmem, vmem),
        scratch_shapes=[
            pltpu.SMEM(table.shape, f32),
            pltpu.SMEM(shifts.shape, f32),
            pltpu.VMEM((cols, 16, width), f32),
            pltpu.VMEM((24, width), jnp.int32),
            pltpu.VMEM((6, 16, width), f32),
            pltpu.VMEM((16, width), f32),
            pltpu.VMEM((8, width), f32),
            pltpu.VMEM((cols * depth, LANES), f32),
            pltpu.VMEM((GROUP, 8, LANES), f32),
            pltpu.VMEM((zs, 8, LANES), f32),
            pltpu.SemaphoreType.REGULAR((7,)),
            dma((2,)), dma, dma((cols,)), dma((2,)), dma((2,)), dma((2, cols)), dma((2, cols)), dma((cols,)), dma((cols,)), dma((2,)), dma((2,)),
            dma((GROUP,)), dma((GROUP,)), dma((zs,)), dma((zs,)),
        ],
        compiler_params=pltpu.CompilerParams(collective_id=0, has_side_effects=True, vmem_limit_bytes=32 * 1024 * 1024),
    )(*(pltpu.with_memory_space_constraint(a, pltpu.HBM) for a in (panel, materials, table, shifts)), shift_pick)
    rows = cols * depth
    basis = pl.pallas_call(
        functools.partial(apply_kernel, cols),
        name="apply",
        out_shape=jax.ShapeDtypeStruct((rows, width), f32),
        in_specs=[vmem] * 3,
        out_specs=hbm,
        scratch_shapes=[pltpu.VMEM((rows, width), f32), pltpu.VMEM((2 * rows, 2 * rows), jnp.bfloat16), dma((4,))],
        compiler_params=pltpu.CompilerParams(vmem_limit_bytes=32 * 1024 * 1024),
    )(inv, w.reshape(rows, width), r.reshape(rows, width))
    return basis.reshape(cols, depth, width)


def solution(mesh):
    placed = (P("fac", "tile", None), P("tile", None), P(), P(), P())
    return jax.shard_map(
        functools.partial(per_device, mesh.shape["tile"]), mesh=mesh, in_specs=placed,
        out_specs=P("fac", "tile", None), check_vma=False,
    )
```

```python
import functools

import jax
import jax.numpy as jnp
from jax import lax
from jax.experimental import pallas as pl
from jax.experimental.pallas import tpu as pltpu
from jax.sharding import PartitionSpec as P

NZ = 64
SWEEPS = 4
OMEGA = 0.8
LANES = 128
YS = 4
CORES = 2
GROUP = 2 * YS * CORES
LINE = YS * CORES
HALO = 4
MESH = pl.DeviceIdType.MESH
HIGHEST = lax.Precision.HIGHEST


def chunked(value):
    return [value[:, i:i + LANES] for i in range(0, value.shape[1], LANES)]


def lane_iota(rows):
    return lax.broadcasted_iota(jnp.int32, (rows, LANES), 1)


def row_iota(rows):
    return lax.broadcasted_iota(jnp.int32, (rows, LANES), 0)


def pick_field(ids, table, field):
    low = (ids & 1) == 1
    mid = (ids & 2) == 2
    high = (ids & 4) == 4
    pairs = [jnp.where(low, table[field, i + 1], table[field, i]) for i in range(0, 8, 2)]
    quads = [jnp.where(mid, pairs[1], pairs[0]), jnp.where(mid, pairs[3], pairs[2])]
    return jnp.where(high, quads[1], quads[0])


def harmonic(first, second):
    return 2.0 * first * second / (first + second)


def plane_faces(ids, table, shift_value):
    count = len(ids)
    lane = lane_iota(8)
    left = lane < NZ
    top = (lane % NZ) == NZ - 1
    cond_y = [pick_field(i, table, 1) for i in ids]
    turned = [pltpu.roll(v, NZ, 1) for v in cond_y]
    faces_y = []
    for k in range(count):
        above = jnp.where(left, turned[k], turned[min(k + 1, count - 1)])
        face = harmonic(cond_y[k], above)
        faces_y.append(jnp.where(left, face, 0.0) if k == count - 1 else face)
    back_y = [pltpu.roll(v, NZ, 1) for v in faces_y]
    found = []
    for k in range(count):
        below = back_y[k - 1] if k else jnp.zeros_like(back_y[0])
        prev_y = jnp.where(left, below, back_y[k])
        cond_z = pick_field(ids[k], table, 2)
        next_z = jnp.where(top, 0.0, harmonic(cond_z, pltpu.roll(cond_z, LANES - 1, 1)))
        prev_z = pltpu.roll(next_z, 1, 1)
        capacity = pick_field(ids[k], table, 3)
        partial = shift_value * capacity + (prev_y + faces_y[k] + prev_z + next_z)
        found.append((prev_y, faces_y[k], prev_z, next_z, partial))
    return found


def own_coefficients(shift_value, ids_ref, table, coef, inv_ref, cond_ref):
    ids = chunked(ids_ref[0:8, :])
    for k, (prev_y, next_y, prev_z, next_z, partial) in enumerate(plane_faces(ids, table, shift_value)):
        where = pl.ds(k * LANES, LANES)
        cond = pick_field(ids[k], table, 0)
        coef[1, 0:8, where] = harmonic(cond, pltpu.roll(cond, 7, 0))
        for i, face in enumerate((prev_y, next_y, prev_z, next_z)):
            coef[2 + i, 0:8, where] = face
        inv_ref[0:8, where] = partial
        cond_ref[:, where] = cond


def all_coefficients(tiles, me, shift_value, ids_ref, table, coef, inv_ref, cond_ref):
    row = row_iota(8)
    after = chunked(ids_ref[8:16, :])
    before = chunked(ids_ref[16:24, :])
    halo = plane_faces([jnp.where(row < HALO, a, b) for a, b in zip(after, before)], table, shift_value)
    for k in range(len(after)):
        where = pl.ds(k * LANES, LANES)
        cond = cond_ref[:, where]
        cond_after = pick_field(after[k], table, 0)
        cond_before = pick_field(before[k], table, 0)
        middle = jnp.where(row < HALO, cond_after, cond_before)
        lower = jnp.where(row < HALO, pltpu.roll(cond_after, 1, 0), pltpu.roll(cond_before, 1, 0))
        lower = jnp.where(row == 0, pltpu.roll(cond, 1, 0), lower)
        upper = jnp.where(row < HALO, pltpu.roll(cond_after, 7, 0), pltpu.roll(cond_before, 7, 0))
        upper = jnp.where(row == 7, pltpu.roll(cond, 7, 0), upper)
        prev_halo = jnp.where((row == 0) & (me == tiles - 1), 0.0, harmonic(lower, middle))
        next_halo = jnp.where((row == 7) & (me == 0), 0.0, harmonic(middle, upper))
        inner = coef[1, 0:8, where]
        next_own = jnp.where(row == 7, pltpu.roll(prev_halo, 7, 0), inner)
        prev_own = jnp.where(row == 0, pltpu.roll(next_halo, 1, 0), pltpu.roll(inner, 1, 0))
        inverse = 1.0 / (inv_ref[0:8, where] + (prev_own + next_own))
        scaled = OMEGA * inverse
        coef[0, 0:8, where] = prev_own * scaled
        coef[1, 0:8, where] = next_own * scaled
        for i in range(2, 6):
            coef[i, 0:8, where] = coef[i, 0:8, where] * scaled
        inv_ref[0:8, where] = inverse
        inverse = 1.0 / (halo[k][4] + (prev_halo + next_halo))
        scaled = OMEGA * inverse
        for i, face in enumerate((prev_halo, next_halo) + halo[k][0:4]):
            coef[i, 8:16, where] = face * scaled
        inv_ref[8:16, where] = inverse


def solve_column(source_ref, coef, inv_ref):
    count = inv_ref.shape[1] // LANES
    where = [pl.ds(k * LANES, LANES) for k in range(count)]
    values = [source_ref[:, where[k]] * inv_ref[:, where[k]] for k in range(count)]
    base = [OMEGA * v for v in values]
    for sweep in range(SWEEPS):
        rows = 8 if sweep == SWEEPS - 1 else 16
        left = lane_iota(rows) < NZ
        centers = [v[0:rows] for v in values]
        turned = [pltpu.roll(v, NZ, 1) for v in centers]
        new = []
        for k in range(count):
            v = centers[k]
            total = (1.0 - OMEGA) * v + base[k][0:rows]
            total += coef[0, 0:rows, where[k]] * pltpu.roll(values[k], 1, 0)[0:rows]
            total += coef[1, 0:rows, where[k]] * pltpu.roll(values[k], 15, 0)[0:rows]
            below = jnp.where(left, turned[max(k - 1, 0)], turned[k])
            above = jnp.where(left, turned[k], turned[min(k + 1, count - 1)])
            total += coef[2, 0:rows, where[k]] * below
            total += coef[3, 0:rows, where[k]] * above
            total += coef[4, 0:rows, where[k]] * pltpu.roll(v, 1, 1)
            total += coef[5, 0:rows, where[k]] * pltpu.roll(v, LANES - 1, 1)
            new.append(total)
        values = new
    return values


def diagonal_blocks(product):
    size = product.shape[0]
    keep = (row_iota(size) % 8) == (lane_iota(size) % 8)
    kept = jnp.where(keep, product, 0.0)
    return jnp.sum(kept.reshape(size // 8, 8, LANES), axis=1)


def thirds(value):
    parts = []
    for _ in range(3):
        part = value.astype(jnp.bfloat16)
        parts.append(part)
        value = value - part.astype(jnp.float32)
    return jnp.concatenate(parts, 0)


def pack(value, first_row, first_column):
    source = lax.broadcasted_iota(jnp.int32, (LANES, LANES), 0)
    target = lax.broadcasted_iota(jnp.int32, (LANES, LANES), 1)
    places = []
    for half in range(2):
        place = (first_row + half * 8) * 4 + first_column + source // 8
        places.append((place == target).astype(jnp.bfloat16))
    left = jnp.concatenate([thirds(value[0:8]), thirds(value[8:16])], 1)
    found = jnp.dot(left, jnp.concatenate(places, 0), preferred_element_type=jnp.float32)
    return found[0:8] + (found[8:16] + found[16:24])


def inverse_factor(packed, size, out):
    count = size // 8
    row = row_iota(8)
    lane = lane_iota(8)

    def spread(value, r):
        return jnp.broadcast_to(value[r:r + 1, :], (8, LANES))

    left = {(j, q): jnp.broadcast_to(packed[:, 32 * q + j:32 * q + j + 1], (8, LANES))
            for j in range(size) for q in range(j // 8, count)}
    right = [jnp.where(lane == row + 8 * q, 1.0, 0.0) for q in range(count)]
    pivots = []
    for k in range(size):
        at, r = k // 8, k % 8
        pivot = 1.0 / spread(left[k, at], r)
        pivots.append(pivot)
        if k == size - 1:
            break
        scaled = {q: left[k, q] * pivot for q in range(at, count)}
        for j in range(k + 1, size):
            other = spread(scaled[j // 8], j % 8)
            for q in range(j // 8, count):
                left[j, q] = left[j, q] - left[k, q] * other
        source = spread(right[at], r)
        for q in range(at, count):
            factor = jnp.where(row > r, scaled[q], 0.0) if q == at else scaled[q]
            right[q] = right[q] - factor * source
    for q in range(count):
        scale = pivots[8 * q]
        for r in range(1, 8):
            scale = jnp.where(row == r, pivots[8 * q + r], scale)
        out[8 * q:8 * q + 8, :] = right[q] * jnp.sqrt(scale)


def solve_kernel(tiles, panel, ids, table_hbm, shifts_hbm, pick, w, r, inv_out, table, shifts,
                 ext, idx, coef, inv_ref, cond, cross, gbuf, zbuf, token,
                 scalar_sem, ids_sem, own_sem, ids_send, ids_recv, halo_send, halo_recv, swap_send, swap_recv, rest_send, rest_recv,
                 group_send, group_recv, line_send, line_recv):
    cols = panel.shape[0]
    width = panel.shape[2]
    half = width // 2
    zs = tiles // LINE
    me = lax.axis_index("tile")
    fac = lax.axis_index("fac")
    parity = fac % 2
    partner = fac + 1 - 2 * parity
    line = me // LINE
    spot = me % LINE
    before = lax.rem(me + tiles - 1, tiles)
    after = lax.rem(me + 1, tiles)
    seat = parity * LINE + spot

    scalars = [pltpu.make_async_copy(a, b, scalar_sem.at[i])
               for i, (a, b) in enumerate(((table_hbm, table), (shifts_hbm, shifts)))]
    own_ids = pltpu.make_async_copy(ids, idx.at[pl.ds(0, 8)], ids_sem)

    def group_peer(step):
        core = lax.rem(spot % CORES + step % CORES, CORES)
        y = lax.rem(spot // CORES + step // CORES % YS, YS)
        x = lax.rem(parity + step // LINE, 2)
        return {"tile": line * LINE + y * CORES + core, "fac": fac - parity + x}, x * LINE + y * CORES + core

    def group_distance(step):
        y = step // CORES % YS
        return step // LINE + min(y, YS - y) + 0.5 * (step % CORES)

    def line_peer(step):
        there = lax.rem(line + step, zs)
        return {"tile": there * LINE + spot, "fac": fac}, there

    def along(distance):
        return {"tile": lax.rem(line + distance + zs, zs) * LINE + spot, "fac": fac}

    barrier = pltpu.get_barrier_semaphore()
    near = {"tile": me, "fac": partner}
    greeted = [{"tile": before, "fac": fac}, {"tile": after, "fac": fac}, near]
    greeted += [{"tile": line * LINE + lax.rem(spot + i, LINE), "fac": fac} for i in range(1, LINE)]
    greeted += [along(i) for i in (-2, -1, 1, 2)]
    for peer in greeted:
        pl.semaphore_signal(barrier, inc=1, device_id=peer, device_id_type=MESH)
    for copy in scalars + [own_ids]:
        copy.start()
    pl.semaphore_wait(barrier, len(greeted))

    def greet(turn):
        pl.semaphore_signal(token.at[2 * turn], inc=1, device_id=along(2), device_id_type=MESH)
        pl.semaphore_signal(token.at[2 * turn + 1], inc=1, device_id=along(-2), device_id_type=MESH)

    def greeted_by(turn):
        pl.semaphore_wait(token.at[2 * turn], 1)
        pl.semaphore_wait(token.at[2 * turn + 1], 1)

    ids_up = pltpu.make_async_remote_copy(ids.at[pl.ds(3, 5)], idx.at[pl.ds(19, 5)], ids_send.at[0], ids_recv.at[0],
                                          device_id={"tile": after, "fac": fac}, device_id_type=MESH)
    ids_down = pltpu.make_async_remote_copy(ids.at[pl.ds(0, 5)], idx.at[pl.ds(8, 5)], ids_send.at[1], ids_recv.at[1],
                                            device_id={"tile": before, "fac": fac}, device_id_type=MESH)
    ids_up.start()
    ids_down.start()

    def halo_up(c):
        return pltpu.make_async_remote_copy(panel.at[c, pl.ds(8 - HALO, HALO)], ext.at[c, pl.ds(8 + HALO, HALO)],
                                            halo_send.at[0, c], halo_recv.at[0, c],
                                            device_id={"tile": after, "fac": fac}, device_id_type=MESH)

    def halo_down(c):
        return pltpu.make_async_remote_copy(panel.at[c, pl.ds(0, HALO)], ext.at[c, pl.ds(8, HALO)],
                                            halo_send.at[1, c], halo_recv.at[1, c],
                                            device_id={"tile": before, "fac": fac}, device_id_type=MESH)

    def own_column(c):
        return pltpu.make_async_copy(panel.at[c], ext.at[c, pl.ds(0, 8)], own_sem.at[c])

    def send_halo(c, carry):
        halo_up(c).start()
        halo_down(c).start()
        own_column(c).start()
        return carry

    lax.fori_loop(0, cols, send_halo, 0)

    giving = pl.ds(pl.multiple_of(parity * half, half), half)

    def swap(c):
        return pltpu.make_async_remote_copy(w.at[c, :, giving], r.at[c, :, giving], swap_send.at[c], swap_recv.at[c],
                                            device_id={"tile": me, "fac": partner}, device_id_type=MESH)

    pl.semaphore_signal(token.at[6], inc=1, device_id=near, device_id_type=MESH)
    greet(0)
    for copy in scalars:
        copy.wait()
    shift_value = shifts[pick[0]]
    own_ids.wait()
    own_coefficients(shift_value, idx, table, coef, inv_ref, cond)
    ids_up.wait()
    ids_down.wait()
    all_coefficients(tiles, me, shift_value, idx, table, coef, inv_ref, cond)

    def column(c, carry):
        halo_up(c).wait()
        halo_down(c).wait()
        own_column(c).wait()

        @pl.when(c > 0)
        def _():
            swap(c - 1).start()

        for turn in range(3):
            @pl.when(c == 4 * (turn + 1))
            def _():
                greeted_by(turn)
                if turn < 2:
                    greet(turn + 1)

        values = solve_column(ext.at[c], coef, inv_ref)
        for k, value in enumerate(values):
            w[c, :, pl.ds(k * LANES, LANES)] = value
        return carry

    lax.fori_loop(0, cols, column, 0)
    def rest(part):
        some = pl.ds(0, cols // 4) if part == 0 else pl.ds(cols // 4, cols - cols // 4)
        side = pl.ds(half, half)
        return pltpu.make_async_remote_copy(w.at[some, :, side], r.at[some, :, side], rest_send.at[part], rest_recv.at[part],
                                            device_id=near, device_id_type=MESH)

    own = w[...].reshape(cols * 8, width)
    gram = lax.dot_general(own, own, (((1,), (1,)), ((), ())), precision=HIGHEST, preferred_element_type=jnp.float32)
    swap(cols - 1).start()

    @pl.when(parity == 0)
    def _():
        rest(0).start()

    own_packed = pack(diagonal_blocks(gram), parity * cols, parity * cols)

    def arrived(c, carry):
        swap(c).wait()
        return carry

    def product(a, b):
        return lax.dot_general(a, b, (((1,), (1,)), ((), ())), precision=HIGHEST, preferred_element_type=jnp.float32)

    early = cols - cols // 4
    for first, last in ((0, early), (early, cols)):
        lax.fori_loop(first, last, arrived, 0)

        @pl.when(parity == 0)
        def _():
            mine = w[:, :, half:].reshape(cols * 8, half)
            cross[8 * first:8 * last, :] = product(r[first:last, :, half:].reshape((last - first) * 8, half), mine)

        @pl.when(parity == 1)
        def _():
            mine = w[:, :, 0:half].reshape(cols * 8, half)
            cross[:, 8 * first:8 * last] = product(mine, r[first:last, :, 0:half].reshape((last - first) * 8, half))

    gbuf[seat] = own_packed + pack(diagonal_blocks(cross[...]), cols, 0)

    def group_copy(step):
        peer, _ = group_peer(step)
        return pltpu.make_async_remote_copy(gbuf.at[seat], gbuf.at[seat], group_send.at[step], group_recv.at[seat],
                                            device_id=peer, device_id_type=MESH)

    def group_arrival(step):
        peer, there = group_peer(step)
        return pltpu.make_async_remote_copy(gbuf.at[there], gbuf.at[there], group_send.at[step], group_recv.at[there],
                                            device_id=peer, device_id_type=MESH)

    def line_copy(step):
        peer, _ = line_peer(step)
        return pltpu.make_async_remote_copy(zbuf.at[line], zbuf.at[line], line_send.at[step], line_recv.at[line],
                                            device_id=peer, device_id_type=MESH)

    def line_arrival(step):
        peer, there = line_peer(step)
        return pltpu.make_async_remote_copy(zbuf.at[there], zbuf.at[there], line_send.at[step], line_recv.at[there],
                                            device_id=peer, device_id_type=MESH)

    pl.semaphore_wait(token.at[6], 1)

    def outward(steps):
        return sorted(steps, key=lambda step: (step >= LINE, group_distance(step)), reverse=True)

    @pl.when(parity == 0)
    def _():
        for step in outward(range(1, GROUP)):
            group_copy(step).start()
        rest(1).start()

    @pl.when(parity == 1)
    def _():
        for step in outward(range(1, LINE)):
            group_copy(step).start()

    for step in range(1, LINE):
        group_arrival(step).wait_recv()

    def group_sum(count):
        total = gbuf[0]
        for i in range(1, count):
            total = total + gbuf[i]
        zbuf[line] = total

    @pl.when(parity == 0)
    def _():
        group_sum(LINE)

    @pl.when(parity == 1)
    def _():
        for step in range(LINE, GROUP):
            group_arrival(step).wait_recv()
        group_sum(GROUP)

    order = sorted(range(1, zs), key=lambda s: -min(s, zs - s))
    for step in order:
        line_copy(step).start()
    for step in range(1, zs):
        line_arrival(step).wait_recv()
    total = zbuf[0]
    for i in range(1, zs):
        total = total + zbuf[i]
    cells = 8 * tiles * width

    @pl.when(parity == 0)
    def _():
        inverse_factor(total / cells, cols, inv_out)

    @pl.when(parity == 1)
    def _():
        inverse_factor(total / cells, 2 * cols, inv_out)

    for step in range(1, LINE):
        group_copy(step).wait_send()
    for step in range(1, zs):
        line_copy(step).wait_send()

    @pl.when(parity == 0)
    def _():
        for step in range(LINE, GROUP):
            group_copy(step).wait_send()
        rest(0).wait_send()
        rest(1).wait_send()

    @pl.when(parity == 1)
    def _():
        rest(0).wait_recv()
        rest(1).wait_recv()


def split(value):
    high = value.astype(jnp.bfloat16)
    low = (value - high.astype(jnp.float32)).astype(jnp.bfloat16)
    return high, low


def dot3(a, b):
    size = a.shape[0] // 2
    high, low = split(b)
    both = jnp.dot(a, high, preferred_element_type=jnp.float32)
    rest = jnp.dot(a[0:size], low, preferred_element_type=jnp.float32)
    return both[0:size] + (both[size:2 * size] + rest)


def apply_kernel(cols, inv, w, r, out, stage, factor, sems):
    parity = lax.axis_index("fac") % 2
    size = cols * 8
    width = w.shape[1]
    block = width // 4
    rows = jnp.where(parity == 0, inv[0:cols, :], inv[cols:2 * cols, :])
    rows = jnp.broadcast_to(rows[:, None, :], (cols, 8, LANES)).reshape(size, LANES)
    source = row_iota(LANES)
    target = lane_iota(LANES)
    same = (source % 8) == (target % 8)
    rows = jnp.concatenate(split(rows), 0)
    same = jnp.concatenate([same, same], 0)
    for part, first in ((0, parity * cols), (1, 0)):
        spread = (source == first + target // 8).astype(jnp.bfloat16)
        wide = jnp.dot(rows, spread, preferred_element_type=jnp.float32)
        factor[:, part * size:(part + 1) * size] = jnp.where(same, wide, 0.0).astype(jnp.bfloat16)

    def send(k):
        part = pl.ds(k * block, block)
        return pltpu.make_async_copy(stage.at[:, part], out.at[:, part], sems.at[k])

    @pl.when(parity == 0)
    def _():
        for k in range(4):
            part = pl.ds(k * block, block)
            stage[:, part] = dot3(factor[:, 0:size], w[:, part])
            send(k).start()

    @pl.when(parity == 1)
    def _():
        for k in range(4):
            part = pl.ds(k * block, block)
            both = jnp.concatenate([w[:, part], r[:, part]], 0)
            stage[:, part] = dot3(factor[...], both)
            send(k).start()

    for k in range(4):
        send(k).wait()


def per_device(tiles, panel, materials, table, shifts, shift_pick):
    cols, depth, width = panel.shape
    zs = tiles // LINE
    hbm = pl.BlockSpec(memory_space=pltpu.HBM)
    vmem = pl.BlockSpec(memory_space=pltpu.VMEM)
    dma = pltpu.SemaphoreType.DMA
    f32 = jnp.float32
    w, r, inv = pl.pallas_call(
        functools.partial(solve_kernel, tiles),
        name="solve",
        out_shape=(jax.ShapeDtypeStruct((cols, depth, width), f32), jax.ShapeDtypeStruct((cols, depth, width), f32),
                   jax.ShapeDtypeStruct((2 * cols, LANES), f32)),
        in_specs=[hbm] * 4 + [pl.BlockSpec(memory_space=pltpu.SMEM)],
        out_specs=(vmem, vmem, vmem),
        scratch_shapes=[
            pltpu.SMEM(table.shape, f32),
            pltpu.SMEM(shifts.shape, f32),
            pltpu.VMEM((cols, 16, width), f32),
            pltpu.VMEM((24, width), jnp.int32),
            pltpu.VMEM((6, 16, width), f32),
            pltpu.VMEM((16, width), f32),
            pltpu.VMEM((8, width), f32),
            pltpu.VMEM((cols * depth, LANES), f32),
            pltpu.VMEM((GROUP, 8, LANES), f32),
            pltpu.VMEM((zs, 8, LANES), f32),
            pltpu.SemaphoreType.REGULAR((7,)),
            dma((2,)), dma, dma((cols,)), dma((2,)), dma((2,)), dma((2, cols)), dma((2, cols)), dma((cols,)), dma((cols,)), dma((2,)), dma((2,)),
            dma((GROUP,)), dma((GROUP,)), dma((zs,)), dma((zs,)),
        ],
        compiler_params=pltpu.CompilerParams(collective_id=0, has_side_effects=True, vmem_limit_bytes=32 * 1024 * 1024),
    )(*(pltpu.with_memory_space_constraint(a, pltpu.HBM) for a in (panel, materials, table, shifts)), shift_pick)
    rows = cols * depth
    basis = pl.pallas_call(
        functools.partial(apply_kernel, cols),
        name="apply",
        out_shape=jax.ShapeDtypeStruct((rows, width), f32),
        in_specs=[vmem] * 3,
        out_specs=hbm,
        scratch_shapes=[pltpu.VMEM((rows, width), f32), pltpu.VMEM((2 * rows, 2 * rows), jnp.bfloat16), dma((4,))],
        compiler_params=pltpu.CompilerParams(vmem_limit_bytes=32 * 1024 * 1024),
    )(inv, w.reshape(rows, width), r.reshape(rows, width))
    return basis.reshape(cols, depth, width)


def solution(mesh):
    placed = (P("fac", "tile", None), P("tile", None), P(), P(), P())
    return jax.shard_map(
        functools.partial(per_device, mesh.shape["tile"]), mesh=mesh, in_specs=placed,
        out_specs=P("fac", "tile", None), check_vma=False,
    )
```
